32 devices in a mesh: rep: 8 (over z, x), atom: 4 (over y, core).
Axes of the slice: x: 2, y: 2, z: 4, core: 2. Of those that a mesh axis runs over, the one named last changes fastest.
Arguments:
- starting_locations: float32 [32, 3, 4096], P('rep', None, 'atom'), may hold values from 0 to 4
- starting_speeds: float32 [32, 3, 4096], P('rep', None, 'atom'), may hold values from -5 to 5
- terminal_location_adjoint: float32 [32, 3, 4096], P('rep', None, 'atom'), may hold values from -6 to 6
- terminal_speed_adjoint: float32 [32, 3, 4096], P('rep', None, 'atom'), may hold values from -7.5 to 7.5
- interaction_strength: float32 [4096], P('atom'), may hold values from 0.5 to 2
- reciprocal_particle_weight: float32 [4096], P('atom'), may hold values from 0.05 to 2
- heat_levels: float32 [32], P('rep'), may hold values from 0.25 to 4
- swap_indicator: int32 [32], P('rep'), may hold values from 0 to 1, as said below
- companion_group_indices: int32 [5, 32, 2], P(None, 'atom'), may hold values from 0 to 23, as said below
Outputs:
- final_pos: float32 [32, 3, 4096], P('rep', None, 'atom')
- final_vel: float32 [32, 3, 4096], P('rep', None, 'atom')
- energies: float32 [32], P('rep')
- grad_pos: float32 [32, 3, 4096], P('rep', None, 'atom')
- grad_vel: float32 [32, 3, 4096], P('rep', None, 'atom')
- grad_coupling: float32 [4096], P('atom')
The draws below stay inside these ranges and needn't reach their ends.
Inputs may be any that keep to these rules, and one draw needn't show every extreme that they name: `swap_indicator`: replicas r and r + 4, for r with r // 4 even, carry the same flag; among the replicas r to r + 3, for r a multiple of 8, at least one carries 1. `companion_group_indices`: the 2 entries of a row differ.
All inputs are finite; a program needn't handle non-finite values.
Results may differ from the reference program's by a relative error of at most 0.0003.
Values sent between devices are 32-bit elements; how exact they have to be, the bound alone decides.
A program may use at most 64 MiB of HBM per device.

```python
import math
import jax
import jax.numpy as jnp
from jax import lax

BLOCK = 128
BLOCKS_DEV = 8
PARTNERS = 2
STEPS = 4
REP_DEV = 4
ATOMS = 4096
WALKER_TOTAL = 32


def draw_starting_locations(key, part):
    grid_shape = (WALKER_TOTAL, ATOMS)
    subkeys = jax.random.split(key, 3)
    inside = jax.random.uniform(subkeys[0], grid_shape)
    owner = (jnp.arange(ATOMS, dtype=jnp.int32) // (BLOCKS_DEV * BLOCK)).astype(jnp.float32)
    along_axis = owner[None, :] + inside
    cross_side = 2.0
    side_axis = jax.random.uniform(subkeys[1], grid_shape) * cross_side
    depth_axis = jax.random.uniform(subkeys[2], grid_shape) * cross_side
    return jnp.stack([along_axis, side_axis, depth_axis], axis=1).astype(jnp.float32)


def motion_noise(key):
    base_key = jax.random.fold_in(key, 101)
    return jnp.clip(jax.random.normal(base_key, (WALKER_TOTAL, 3, ATOMS)), -5.0, 5.0)


def draw_starting_speeds(key, part):
    return motion_noise(key).astype(jnp.float32)


def draw_terminal_speed_adjoint(key, part):
    fresh_noise = jnp.clip(jax.random.normal(jax.random.fold_in(key, 202), (WALKER_TOTAL, 3, ATOMS)), -5.0, 5.0)
    return (0.5 * motion_noise(key) + fresh_noise).astype(jnp.float32)


def draw_reciprocal_particle_weight(key, part):
    ramp_up = jnp.arange(ATOMS, dtype=jnp.float32) / ATOMS
    roughness = jnp.exp(jax.random.uniform(key, (ATOMS,), minval=jnp.log(0.5), maxval=jnp.log(2.0)))
    return (roughness / (1.0 + 2.0 * ramp_up)).astype(jnp.float32)


def draw_swap_indicator(key, part):
    groups = WALKER_TOTAL // (2 * REP_DEV)
    flag_key = jax.random.fold_in(key, 303)
    slot_key = jax.random.fold_in(key, 404)
    base_flags = jax.random.randint(flag_key, (groups, REP_DEV), 0, 2)
    forced_slot = jax.random.randint(slot_key, (groups, 1), 0, REP_DEV)
    forced = (jnp.arange(REP_DEV, dtype=jnp.int32)[None, :] == forced_slot).astype(jnp.int32)
    base_flags = jnp.maximum(base_flags, forced)
    spread = jnp.broadcast_to(base_flags[:, None, :], (groups, 2, REP_DEV))
    return spread.reshape(WALKER_TOTAL).astype(jnp.int32)


def draw_companion_group_indices(key, part):
    slot_count = 3 * BLOCKS_DEV
    scores = jax.random.randint(key, (STEPS + 1, ATOMS // BLOCK, slot_count), 0, 1 << 20)
    scores = scores * slot_count + jnp.arange(slot_count, dtype=jnp.int32)
    return lax.top_k(scores, PARTNERS)[1].astype(jnp.int32)


def level_of(own_key, dims, cuts, smallest, top_value):
    def one(axis_at, blocks):
        heights = jax.random.uniform(jax.random.fold_in(jax.random.fold_in(own_key, 6), axis_at), (blocks,), jnp.float32, smallest / len(cuts), top_value / len(cuts))
        return jnp.repeat(jnp.exp(heights), dims[axis_at] // blocks).reshape((-1,) + (1,) * (len(dims) - axis_at - 1))

    factor_of = one(*cuts[0])
    for cut in cuts[1:]:
        factor_of = factor_of * one(*cut)
    return factor_of


def noise(stream_key, dims, deviation, limit, pieces=(), kind=jnp.bfloat16):
    drawn = deviation * jax.random.normal(stream_key, dims, jnp.float32)
    if pieces:
        drawn = drawn * level_of(stream_key, dims, pieces, -0.22, 0.18)
    return jnp.clip(drawn, -limit, limit).astype(kind)


def setup_inputs(seed: int = 0) -> dict:
    arg_keys = jax.random.split(jax.random.key(seed), 10)
    return {
        "starting_locations": draw_starting_locations(jax.random.fold_in(arg_keys[9], 71), 0),
        "starting_speeds": draw_starting_speeds(jax.random.fold_in(arg_keys[9], 71), 0),
        "terminal_location_adjoint": noise(arg_keys[2], (WALKER_TOTAL, 3, ATOMS), 1.0, 6.0, ((0, 8), (2, 4)), jnp.float32),
        "terminal_speed_adjoint": draw_terminal_speed_adjoint(jax.random.fold_in(arg_keys[9], 71), 0),
        "interaction_strength": jnp.clip(jnp.exp(math.log(2.0) - 1.3862944 * jax.random.uniform(arg_keys[4], (ATOMS,), jnp.float32) ** level_of(arg_keys[4], (ATOMS,), ((0, 4),), -0.2, 0.2)), 0.5, 2.0),
        "reciprocal_particle_weight": draw_reciprocal_particle_weight(jax.random.fold_in(arg_keys[9], 71), 0),
        "heat_levels": jnp.clip(jnp.exp(math.log(4.0) - 2.7725887 * jax.random.uniform(arg_keys[6], (WALKER_TOTAL,), jnp.float32) ** level_of(arg_keys[6], (WALKER_TOTAL,), ((0, 8),), -0.2, 0.2)), 0.25, 4.0),
        "swap_indicator": draw_swap_indicator(jax.random.fold_in(arg_keys[9], 71), 0),
        "companion_group_indices": draw_companion_group_indices(jax.random.fold_in(arg_keys[9], 71), 0),
    }


TIME_STEP = 0.05
THERMO_RELAX = 0.5
KINETIC_EPSILON = 1e-06

def walker_energy(particle_location, interaction_strength, lists_now):
    padding = BLOCKS_DEV * BLOCK
    block_total = ATOMS // BLOCK
    padded_pos = jnp.pad(particle_location, ((0, 0), (padding, padding))).reshape(3, block_total + 2 * BLOCKS_DEV, BLOCK)
    padded_coupling = jnp.pad(interaction_strength, (padding, padding)).reshape(block_total + 2 * BLOCKS_DEV, BLOCK)
    block_ids = jnp.arange(block_total, dtype=jnp.int32)
    chosen = (block_ids // BLOCKS_DEV * BLOCKS_DEV)[:, None] + lists_now
    own_block = particle_location.reshape(3, block_total, BLOCK)
    far_block = padded_pos[:, chosen]
    squared = jnp.zeros((block_total, PARTNERS, BLOCK, BLOCK), particle_location.dtype)
    for axis_id in range(3):
        offset = own_block[axis_id][:, None, :, None] - far_block[axis_id][:, :, None, :]
        squared = squared + offset * offset
    self_block = lists_now == (BLOCKS_DEV + block_ids % BLOCKS_DEV)[:, None]
    diagonal = jnp.arange(BLOCK)[:, None] == jnp.arange(BLOCK)[None, :]
    kept_pairs = 1.0 - (self_block[:, :, None, None] & diagonal).astype(particle_location.dtype)
    weight = interaction_strength.reshape(block_total, BLOCK)[:, None, :, None] * padded_coupling[chosen][:, :, None, :]
    strength = BLOCKS_DEV / (8.0 * PARTNERS)
    return 0.5 * strength * jnp.sum(weight * jnp.exp(-0.5 * squared) * kept_pairs)

def force_and_energy(particle_location, interaction_strength, lists_now):
    energy, gradient = jax.value_and_grad(walker_energy)(particle_location, interaction_strength, lists_now)
    return (-gradient, energy)

def trajectory(opening_location, opening_speed, interaction_strength, reciprocal_particle_weight, companion_group_indices, leading_heat_level, trailing_heat_level):
    stepper = jax.checkpoint(force_and_energy)
    half_step = 0.5 * TIME_STEP
    push_vectors, energy = stepper(opening_location, interaction_strength, companion_group_indices[0])
    particle_location, particle_speed, desired_heat_level = (opening_location, opening_speed, leading_heat_level)
    for iteration_number in range(STEPS):
        if iteration_number == STEPS // 2:
            particle_speed = particle_speed * jnp.sqrt(trailing_heat_level / leading_heat_level)
            desired_heat_level = trailing_heat_level
        mid_velocity = particle_speed + half_step * reciprocal_particle_weight * push_vectors
        particle_location = particle_location + TIME_STEP * mid_velocity
        push_vectors, energy = stepper(particle_location, interaction_strength, companion_group_indices[iteration_number + 1])
        updated = mid_velocity + half_step * reciprocal_particle_weight * push_vectors
        kinetic = 0.5 * jnp.sum(updated * updated / reciprocal_particle_weight)
        present_state = 2.0 * kinetic / (3 * ATOMS) + KINETIC_EPSILON
        rescaling_multiplier = jnp.sqrt(1.0 + THERMO_RELAX * (desired_heat_level / present_state - 1.0))
        particle_speed = rescaling_multiplier * updated
    return ((particle_location, particle_speed), energy / ATOMS)

def reference(starting_locations, starting_speeds, terminal_location_adjoint, terminal_speed_adjoint, interaction_strength, reciprocal_particle_weight, heat_levels, swap_indicator, companion_group_indices):
    walker_ids = jnp.arange(WALKER_TOTAL, dtype=jnp.int32)
    swap_companion = jnp.where(walker_ids // REP_DEV % 2 == 0, walker_ids + REP_DEV, walker_ids - REP_DEV)
    upcoming_heat_level = jnp.where(swap_indicator == 1, heat_levels[swap_companion], heat_levels)

    def lone_walker(collapsed_total, sliced):
        walker_pos, walker_vel, leading_heat_level, trailing_heat_level, walker_cot_pos, walker_cot_vel = sliced

        def rollout(particle_location, particle_speed, couplings):
            return trajectory(particle_location, particle_speed, couplings, reciprocal_particle_weight, companion_group_indices, leading_heat_level, trailing_heat_level)
        finals, pullback, energy = jax.vjp(rollout, walker_pos, walker_vel, interaction_strength, has_aux=True)
        grad_position, grad_velocity, grad_couplings = pullback((walker_cot_pos, walker_cot_vel))
        return (collapsed_total + grad_couplings, (finals[0], finals[1], energy, grad_position, grad_velocity))
    collapsed_total, gathered_results = lax.scan(lone_walker, jnp.zeros_like(interaction_strength), (starting_locations, starting_speeds, heat_levels, upcoming_heat_level, terminal_location_adjoint, terminal_speed_adjoint))
    return (gathered_results[0], gathered_results[1], gathered_results[2], gathered_results[3], gathered_results[4], collapsed_total)
```

```python
import functools
import math

import jax
import jax.numpy as jnp
from jax import lax
from jax.experimental import pallas as pl
from jax.experimental.pallas import tpu as pltpu
from jax.sharding import PartitionSpec as P

TIME_STEP = 0.05
THERMO_RELAX = 0.5
KINETIC_EPSILON = 1e-06


def with_halo(block, sides, width):
    for axis, dim in sides:
        count = lax.axis_size(axis)
        forward = [(i, i + 1) for i in range(count - 1)]
        backward = [(target, source) for source, target in forward]
        low = lax.ppermute(
            lax.slice_in_dim(block, block.shape[dim] - width, None, axis=dim), axis, forward
        )
        high = lax.ppermute(lax.slice_in_dim(block, 0, width, axis=dim), axis, backward)
        block = jnp.concatenate([low, block, high], axis=dim)
    return block


def from_partner(x, axis, apart):
    return lax.ppermute(x, axis, [(i, i ^ 1 << apart) for i in range(lax.axis_size(axis))])


def split_blocks(extended, block_count):
    block_width = extended.shape[2] // (3 * block_count)
    return extended.reshape(extended.shape[0], 4, 3 * block_count, block_width)


def pair_terms(blocks, own_start, far_ids, keep):
    block_count = far_ids.shape[0]
    partners = far_ids.shape[1]
    block_width = blocks.shape[3]
    own_block = blocks[:, :, own_start : own_start + block_count]
    far_block = jnp.take(blocks, far_ids, axis=2)
    squared = jnp.zeros(
        (blocks.shape[0], block_count, partners, block_width, block_width), jnp.float32
    )
    for axis_id in range(3):
        offset = own_block[:, axis_id, :, None, :, None] - far_block[:, axis_id, :, :, None, :]
        squared = squared + offset * offset
    own_ids = own_start + jnp.arange(block_count, dtype=jnp.int32)
    self_block = far_ids == own_ids[:, None]
    diagonal = jnp.arange(block_width)[:, None] == jnp.arange(block_width)[None, :]
    kept_pairs = keep[:, :, None, None] * (
        1.0 - (self_block[:, :, None, None] & diagonal).astype(jnp.float32)
    )
    weight = own_block[:, 3, :, None, :, None] * far_block[:, 3, :, :, None, :]
    strength = block_count / (8.0 * partners)
    return (
        0.5 * strength * jnp.sum(weight * jnp.exp(-0.5 * squared) * kept_pairs, axis=(1, 2, 3, 4))
    )


def energy_of(extended, companion_group_indices, beside_all, iteration_number):
    lists_now = companion_group_indices[iteration_number]
    block_count = lists_now.shape[0]
    blocks = split_blocks(extended, block_count)
    per_walker = pair_terms(blocks, block_count, lists_now, jnp.ones(lists_now.shape, jnp.float32))
    total = jnp.sum(per_walker)
    return (total, per_walker)


def widen(layer):
    return with_halo(layer, (("atom", 2),), layer.shape[2])


def settle(gradient):
    block_width = gradient.shape[2] // 3
    padded = with_halo(gradient, (("atom", 2),), block_width)
    return (
        padded[:, :, 2 * block_width : 3 * block_width]
        + padded[:, :, :block_width]
        + padded[:, :, 4 * block_width :]
    )


def atom_total(partial_value):
    return lax.psum(partial_value, "atom")


def force_from(particle_location, interaction_strength, companion_group_indices, iteration_number):
    column = jnp.broadcast_to(
        interaction_strength[None, None, :],
        (particle_location.shape[0], 1, particle_location.shape[2]),
    )
    extended = widen(jnp.concatenate([particle_location, column], axis=1))
    (collapsed_total, per_walker), gradient = jax.value_and_grad(energy_of, has_aux=True)(
        extended, companion_group_indices, None, iteration_number
    )
    return (-settle(gradient[:, :3]), per_walker, extended)


def force_back(cot_force, extended, companion_group_indices, iteration_number):

    def slope_of(widened):
        return jax.grad(energy_of, has_aux=True)(
            widened, companion_group_indices, None, iteration_number
        )[0][:, :3]

    slope_now, pullback = jax.vjp(slope_of, extended)
    cot_extended = pullback(-widen(cot_force))[0]
    returned = settle(cot_extended)
    return (returned[:, :3], jnp.sum(returned[:, 3], axis=0))


def local_general(
    starting_locations,
    starting_speeds,
    terminal_location_adjoint,
    terminal_speed_adjoint,
    interaction_strength,
    reciprocal_particle_weight,
    heat_levels,
    swap_indicator,
    companion_group_indices,
):
    half_step = 0.5 * TIME_STEP
    atoms_all = starting_locations.shape[2] * lax.axis_size("atom")
    mass_row = reciprocal_particle_weight[None, None, :]
    steps_all = companion_group_indices.shape[0] - 1
    swap_at = steps_all // 2
    push_vectors, energy, extended = force_from(
        starting_locations, interaction_strength, companion_group_indices, 0
    )
    saved_extended = [extended]
    saved_updated = []
    saved_factor = []
    saved_current = []
    stored_goal = []
    particle_location, particle_speed = (starting_locations, starting_speeds)
    desired_heat_level = heat_levels
    partner_temp = from_partner(heat_levels, "rep", 0)
    upcoming_heat_level = jnp.where(swap_indicator == 1, partner_temp, heat_levels)
    interaction_multiplier = jnp.sqrt(upcoming_heat_level / heat_levels)[:, None, None]
    for iteration_number in range(steps_all):
        if iteration_number == swap_at:
            particle_speed = particle_speed * interaction_multiplier
            desired_heat_level = upcoming_heat_level
        mid_velocity = particle_speed + half_step * mass_row * push_vectors
        particle_location = particle_location + TIME_STEP * mid_velocity
        push_vectors, energy, extended = force_from(
            particle_location, interaction_strength, companion_group_indices, iteration_number + 1
        )
        updated = mid_velocity + half_step * mass_row * push_vectors
        kinetic, energy = atom_total(
            (0.5 * jnp.sum(updated * updated / mass_row, axis=(1, 2)), energy)
        )
        present_state = 2.0 * kinetic / (3 * atoms_all) + KINETIC_EPSILON
        rescaling_multiplier = jnp.sqrt(
            1.0 + THERMO_RELAX * (desired_heat_level / present_state - 1.0)
        )
        particle_speed = rescaling_multiplier[:, None, None] * updated
        saved_extended.append(extended)
        saved_updated.append(updated)
        saved_factor.append(rescaling_multiplier)
        saved_current.append(present_state)
        stored_goal.append(desired_heat_level)
    energies = energy / atoms_all
    cot_x, cot_v = (terminal_location_adjoint, terminal_speed_adjoint)
    cot_f = jnp.zeros_like(cot_x)
    cot_coupling = jnp.zeros_like(interaction_strength)
    for iteration_number in reversed(range(steps_all)):
        updated = saved_updated[iteration_number]
        rescaling_multiplier = saved_factor[iteration_number]
        present_state = saved_current[iteration_number]
        desired_heat_level = stored_goal[iteration_number]
        inner_sum = atom_total(jnp.sum(cot_v * updated, axis=(1, 2)))
        slope_factor = (
            -THERMO_RELAX
            * desired_heat_level
            / (present_state * present_state)
            * (2.0 / (3 * atoms_all))
            / (2.0 * rescaling_multiplier)
        )
        cot_updated = (
            rescaling_multiplier[:, None, None] * cot_v
            + (inner_sum * slope_factor)[:, None, None] * updated / mass_row
        )
        cot_force_now = cot_f + half_step * mass_row * cot_updated
        returned_x, returned_c = force_back(
            cot_force_now,
            saved_extended[iteration_number + 1],
            companion_group_indices,
            iteration_number + 1,
        )
        cot_coupling = cot_coupling + returned_c
        cot_x = cot_x + returned_x
        cot_mid = cot_updated + TIME_STEP * cot_x
        cot_v = cot_mid
        cot_f = half_step * mass_row * cot_mid
        if iteration_number == swap_at:
            cot_v = cot_v * interaction_multiplier
    returned_x, returned_c = force_back(cot_f, saved_extended[0], companion_group_indices, 0)
    cot_x = cot_x + returned_x
    cot_coupling = cot_coupling + returned_c
    grad_coupling = lax.psum(cot_coupling, "rep")
    return (particle_location, particle_speed, energies, cot_x, cot_v, grad_coupling)


LOG2E = math.log2(math.e)
ROWS = 16
KDIST = 32
KCROSS = 48
UNROLL = 4


def split3(x):
    hi = x.astype(jnp.bfloat16).astype(jnp.float32)
    rest = x - hi
    mid = rest.astype(jnp.bfloat16).astype(jnp.float32)
    low = (rest - mid).astype(jnp.bfloat16).astype(jnp.float32)
    return hi, mid, low


def row_sum(x):
    return jnp.sum(x, axis=1, keepdims=True)


def whole_sum(x):
    return jnp.full((1, x.shape[-1]), jnp.sum(x), jnp.float32)


def replica_kernel(
    far_ref,
    temp_ref,
    x0_ref,
    v0_ref,
    cx_ref,
    cv_ref,
    c_ref,
    m_ref,
    xf_ref,
    vf_ref,
    en_ref,
    gx_ref,
    gv_ref,
    gc_ref,
    left,
    right,
    left_w,
    right_w,
    rows_w,
    rows_x,
    rows_g,
    weights,
    acc_w,
    acc_v,
    out_w,
    out_v,
    saved_u,
    f_ref,
    fac_ref,
    cur_ref,
):
    nb, _, width = x0_ref.shape
    evals = rows_x.shape[0]
    steps = evals - 1
    partners = 2
    half = 0.5 * TIME_STEP
    block_count = temp_ref[2]
    dof = float(3 * nb * width)
    f32, bf16 = jnp.float32, jnp.bfloat16
    real = slice(0, nb)
    t_first = jnp.full((1, width), temp_ref[0], f32)
    t_last = jnp.full((1, width), temp_ref[1], f32)
    swap_gain = jnp.sqrt(t_last / t_first)
    strength = 0.5 * block_count / (8.0 * partners)
    log_scale = jnp.log(strength * jnp.ones((1, width), f32)) * LOG2E
    mass = m_ref[...]

    for ref in (left_w, right_w, rows_w):
        ref[...] = jnp.zeros_like(ref)
    rows_x[...] = jnp.zeros_like(rows_x)
    rows_g[...] = jnp.zeros_like(rows_g)

    def put(ref, at, value):
        ref[real, at : at + value.shape[1], :] = value

    one = jnp.ones((nb, 1, width), f32)
    zero_pad = (((0,), (0,)), ((), ()))

    def pair(ref, n, p):
        base = (n * nb + p) * partners
        return jnp.concatenate([ref[far_ref[base]], ref[far_ref[base + 1]]], axis=1)

    def scatter(out, acc, n):
        for p in range(nb):
            base = (n * nb + p) * partners
            for k in range(partners):
                q = far_ref[base + k]
                acc[q] = acc[q] + out[p, :, k * width : (k + 1) * width]

    def set_rows(dest, value):
        hi, mid, low = split3(value)
        put(rows_w, 0, hi)
        put(rows_w, 3, mid)
        put(rows_w, 6, low)
        put(rows_w, 9, one)
        dest[...] = rows_w[...].astype(bf16)

    def products(first, second, at):
        for i, j in ((0, 0), (0, 1), (1, 0), (0, 2), (1, 1), (2, 0)):
            put(left_w, at, first[i])
            put(right_w, at, second[j])
            at += first[0].shape[1]
        return at

    def singles(ref, other, value, at):
        for part in split3(value):
            put(ref, at, part)
            put(other, at, one)
            at += 1
        return at

    def force(x, n):
        set_rows(rows_x.at[n], x)
        self_term = -0.5 * LOG2E * row_sum(x * x) + jnp.log(c_ref[...]) * LOG2E
        at = products(split3(x * LOG2E), split3(x), 0)
        at = singles(left_w, right_w, self_term + log_scale, at)
        at = singles(right_w, left_w, self_term, at)
        right_w[nb, at - 3 : at - 2, :] = jnp.full((1, width), -1e6, f32)
        left[:, 0:KDIST, :] = left_w[real, 0:KDIST, :].astype(bf16)
        right[:, 0:KDIST, :] = right_w[:, 0:KDIST, :].astype(bf16)

        @pl.loop(0, nb // UNROLL)
        def _(chunk):
            for i in range(UNROLL):
                p = chunk * UNROLL + i
                exponent = lax.dot_general(
                    left[p, 0:KDIST, :],
                    pair(right.at[:, 0:KDIST, :], n, p),
                    zero_pad,
                    preferred_element_type=f32,
                )
                w = jnp.exp2(exponent).astype(bf16)
                weights[n, p] = w
                out_w[p] = jnp.dot(rows_x[n, p], w, preferred_element_type=f32)
                acc_w[p] = lax.dot_general(
                    pair(rows_x.at[n], n, p),
                    w,
                    (((1,), (1,)), ((), ())),
                    preferred_element_type=f32,
                )

        scatter(out_w, acc_w, n)
        pulled = acc_w[real, 0:3, :] + acc_w[real, 3:6, :] + acc_w[real, 6:9, :]
        f_ref[...] = x * acc_w[real, 9:10, :] - pulled

    def force_back(g, n):
        x = (
            rows_x[n, real].astype(f32)[:, 0:3]
            + rows_x[n, real].astype(f32)[:, 3:6]
            + rows_x[n, real].astype(f32)[:, 6:9]
        )
        set_rows(rows_g, g)
        sx, sg = split3(x), split3(g)
        neg_g = tuple(-part for part in sg)
        neg_x = tuple(-part for part in sx)
        at = products(sx, neg_g, 0)
        at = products(sg, neg_x, at)
        own = row_sum(x * g)
        at = singles(left_w, right_w, own, at)
        singles(right_w, left_w, own, at)
        left[...] = left_w[real].astype(bf16)
        right[...] = right_w[...].astype(bf16)

        @pl.loop(0, nb // UNROLL)
        def _(chunk):
            for i in range(UNROLL):
                p = chunk * UNROLL + i
                phi = lax.dot_general(
                    left[p], pair(right, n, p), zero_pad, preferred_element_type=f32
                )
                w = weights[n, p]
                v = (w.astype(f32) * phi).astype(bf16)
                out_w[p] = jnp.dot(rows_g[p], w, preferred_element_type=f32)
                out_v[p] = jnp.dot(rows_x[n, p], v, preferred_element_type=f32)
                acc_w[p] = lax.dot_general(
                    pair(rows_g, n, p),
                    w,
                    (((1,), (1,)), ((), ())),
                    preferred_element_type=f32,
                )
                acc_v[p] = lax.dot_general(
                    pair(rows_x.at[n], n, p),
                    v,
                    (((1,), (1,)), ((), ())),
                    preferred_element_type=f32,
                )

        scatter(out_w, acc_w, n)
        scatter(out_v, acc_v, n)
        pulled_w = acc_w[real, 0:3, :] + acc_w[real, 3:6, :] + acc_w[real, 6:9, :]
        pulled_v = acc_v[real, 0:3, :] + acc_v[real, 3:6, :] + acc_v[real, 6:9, :]
        total_v = acc_v[real, 9:10, :]
        back_x = g * acc_w[real, 9:10, :] - pulled_w - x * total_v + pulled_v
        return back_x, total_v

    x, v, goal = x0_ref[...], v0_ref[...], t_first
    force(x, 0)
    for n in range(steps):
        if n == steps // 2:
            v = v * swap_gain
            goal = t_last
        mid = v + half * mass * f_ref[...]
        x = x + TIME_STEP * mid
        force(x, n + 1)
        u = mid + half * mass * f_ref[...]
        kinetic = 0.5 * whole_sum(u * u / mass)
        current = 2.0 * kinetic / dof + KINETIC_EPSILON
        factor = jnp.sqrt(1.0 + THERMO_RELAX * (goal / current - 1.0))
        v = factor * u
        saved_u[n] = u
        fac_ref[n] = factor
        cur_ref[n] = current
    xf_ref[...] = x
    vf_ref[...] = v
    coupling = c_ref[...]
    selfs = jnp.zeros((1, width), f32)
    square = strength * jnp.sum(coupling * coupling, axis=1)
    owned = jnp.zeros((1, width), f32)
    for p in range(nb):
        base = (steps * nb + p) * partners
        for k in range(partners):
            hit = (far_ref[base + k] == p).astype(f32)
            selfs = selfs + hit * square[p : p + 1]
    total = whole_sum(acc_w[real, 9:10, :]) * 0.5 - whole_sum(selfs)
    en_ref[...] = total / float(nb * width)

    cot_x, cot_v = cx_ref[...], cv_ref[...]
    cot_f = jnp.zeros_like(cot_x)
    cot_c = jnp.zeros((nb, 1, width), f32)
    for n in reversed(range(steps)):
        goal = t_last if n >= steps // 2 else t_first
        u, factor, current = saved_u[n], fac_ref[n], cur_ref[n]
        inner = whole_sum(cot_v * u)
        slope = -THERMO_RELAX * goal / (current * current) * (2.0 / dof) / (2.0 * factor)
        cot_u = factor * cot_v + (inner * slope) * u / mass
        back_x, back_c = force_back(cot_f + half * mass * cot_u, n + 1)
        cot_c = cot_c + back_c
        cot_x = cot_x + back_x
        cot_mid = cot_u + TIME_STEP * cot_x
        cot_v = cot_mid
        cot_f = half * mass * cot_mid
        if n == steps // 2:
            cot_v = cot_v * swap_gain
    back_x, back_c = force_back(cot_f, 0)
    gx_ref[...] = cot_x + back_x
    gv_ref[...] = cot_v
    gc_ref[...] = (cot_c + back_c) / coupling


def run_replica(far, temps, x0, v0, cx, cv, coupling, mass, evals):
    nb, _, width = x0.shape
    f32, bf16 = jnp.float32, jnp.bfloat16
    vec = jax.ShapeDtypeStruct((nb, 3, width), f32)
    vmem = pl.BlockSpec(memory_space=pltpu.VMEM)
    smem = pl.BlockSpec(memory_space=pltpu.SMEM)
    return pl.pallas_call(
        replica_kernel,
        out_shape=(
            vec,
            vec,
            jax.ShapeDtypeStruct((1, width), f32),
            vec,
            vec,
            jax.ShapeDtypeStruct((nb, 1, width), f32),
        ),
        in_specs=[smem, smem] + [vmem] * 6,
        out_specs=[vmem] * 6,
        scratch_shapes=[
            pltpu.VMEM((nb, KCROSS, width), bf16),
            pltpu.VMEM((nb + 1, KCROSS, width), bf16),
            pltpu.VMEM((nb + 1, KCROSS, width), f32),
            pltpu.VMEM((nb + 1, KCROSS, width), f32),
            pltpu.VMEM((nb + 1, ROWS, width), f32),
            pltpu.VMEM((evals, nb + 1, ROWS, width), bf16),
            pltpu.VMEM((nb + 1, ROWS, width), bf16),
            pltpu.VMEM((evals, nb, width, 2 * width), bf16),
            pltpu.VMEM((nb + 1, ROWS, width), f32),
            pltpu.VMEM((nb + 1, ROWS, width), f32),
            pltpu.VMEM((nb, ROWS, 2 * width), f32),
            pltpu.VMEM((nb, ROWS, 2 * width), f32),
            pltpu.VMEM((evals - 1, nb, 3, width), f32),
            pltpu.VMEM((nb, 3, width), f32),
            pltpu.VMEM((evals - 1, 1, width), f32),
            pltpu.VMEM((evals - 1, 1, width), f32),
        ],
        compiler_params=pltpu.CompilerParams(vmem_limit_bytes=60 * 1024 * 1024),
    )(far, temps, x0, v0, cx, cv, coupling, mass)


def local_whole(
    starting_locations,
    starting_speeds,
    terminal_location_adjoint,
    terminal_speed_adjoint,
    interaction_strength,
    reciprocal_particle_weight,
    heat_levels,
    swap_indicator,
    companion_group_indices,
):
    evals, blocks, partners = companion_group_indices.shape
    owners = lax.axis_size("atom")
    me = lax.axis_index("atom")
    atoms = starting_locations.shape[2]
    width = atoms // blocks
    nb = owners * blocks
    packed = jnp.concatenate(
        [
            starting_locations,
            starting_speeds,
            terminal_location_adjoint,
            terminal_speed_adjoint,
        ],
        axis=1,
    )
    mine = lax.all_to_all(packed, "atom", 0, 0, tiled=True)
    mine = mine.reshape(owners, 12, blocks, width).transpose(0, 2, 1, 3).reshape(nb, 12, width)
    shared = lax.all_gather(
        jnp.stack([interaction_strength, reciprocal_particle_weight]), "atom", axis=0
    )
    coupling = shared[:, 0].reshape(nb, 1, width)
    mass = shared[:, 1].reshape(nb, 1, width)
    slots = lax.all_gather(companion_group_indices, "atom", axis=1, tiled=True)
    block_ids = jnp.arange(nb, dtype=jnp.int32)
    far = (block_ids // blocks * blocks - blocks)[None, :, None] + slots
    far = jnp.where((far >= 0) & (far < nb), far, nb).reshape(-1)
    partner_temp = from_partner(heat_levels, "rep", 0)
    upcoming = jnp.where(swap_indicator == 1, partner_temp, heat_levels)
    temps = jnp.stack(
        [
            lax.dynamic_index_in_dim(heat_levels, me, keepdims=False),
            lax.dynamic_index_in_dim(upcoming, me, keepdims=False),
            jnp.float32(blocks),
        ]
    )
    xf, vf, en, gx, gv, gc = run_replica(
        far,
        temps,
        mine[:, 0:3],
        mine[:, 3:6],
        mine[:, 6:9],
        mine[:, 9:12],
        coupling,
        mass,
        evals,
    )
    done = jnp.concatenate([xf, vf, gx, gv], axis=1)
    done = done.reshape(owners, blocks, 12, width).transpose(0, 2, 1, 3).reshape(owners, 12, atoms)
    done = lax.all_to_all(done, "atom", 0, 0, tiled=True)
    energies = lax.all_gather(en[0, 0:1], "atom", axis=0, tiled=True)
    part = lax.psum_scatter(gc.reshape(-1), "atom", scatter_dimension=0, tiled=True)
    grad_coupling = lax.psum(part, "rep")
    return (done[:, 0:3], done[:, 3:6], energies, done[:, 6:9], done[:, 9:12], grad_coupling)


def local(*args):
    partners = args[8].shape[2]
    if args[0].shape[0] == lax.axis_size("atom") and partners == 2:
        return local_whole(*args)
    return local_general(*args)


def solution(mesh):
    in_specs = (
        P("rep", None, "atom"),
        P("rep", None, "atom"),
        P("rep", None, "atom"),
        P("rep", None, "atom"),
        P("atom"),
        P("atom"),
        P("rep"),
        P("rep"),
        P(None, "atom", None),
    )
    out_specs = (
        P("rep", None, "atom"),
        P("rep", None, "atom"),
        P("rep"),
        P("rep", None, "atom"),
        P("rep", None, "atom"),
        P("atom"),
    )
    return jax.shard_map(local, mesh=mesh, in_specs=in_specs, out_specs=out_specs, check_vma=False)
```

```python
import functools
import math

import jax
import jax.numpy as jnp
from jax import lax
from jax.experimental import pallas as pl
from jax.experimental.pallas import tpu as pltpu
from jax.sharding import PartitionSpec as P

TIME_STEP = 0.05
THERMO_RELAX = 0.5
KINETIC_EPSILON = 1e-06


def with_halo(block, sides, width):
    for axis, dim in sides:
        count = lax.axis_size(axis)
        forward = [(i, i + 1) for i in range(count - 1)]
        backward = [(target, source) for source, target in forward]
        low = lax.ppermute(
            lax.slice_in_dim(block, block.shape[dim] - width, None, axis=dim), axis, forward
        )
        high = lax.ppermute(lax.slice_in_dim(block, 0, width, axis=dim), axis, backward)
        block = jnp.concatenate([low, block, high], axis=dim)
    return block


def from_partner(x, axis, apart):
    return lax.ppermute(x, axis, [(i, i ^ 1 << apart) for i in range(lax.axis_size(axis))])


def split_blocks(extended, block_count):
    block_width = extended.shape[2] // (3 * block_count)
    return extended.reshape(extended.shape[0], 4, 3 * block_count, block_width)


def pair_terms(blocks, own_start, far_ids, keep):
    block_count = far_ids.shape[0]
    partners = far_ids.shape[1]
    block_width = blocks.shape[3]
    own_block = blocks[:, :, own_start : own_start + block_count]
    far_block = jnp.take(blocks, far_ids, axis=2)
    squared = jnp.zeros(
        (blocks.shape[0], block_count, partners, block_width, block_width), jnp.float32
    )
    for axis_id in range(3):
        offset = own_block[:, axis_id, :, None, :, None] - far_block[:, axis_id, :, :, None, :]
        squared = squared + offset * offset
    own_ids = own_start + jnp.arange(block_count, dtype=jnp.int32)
    self_block = far_ids == own_ids[:, None]
    diagonal = jnp.arange(block_width)[:, None] == jnp.arange(block_width)[None, :]
    kept_pairs = keep[:, :, None, None] * (
        1.0 - (self_block[:, :, None, None] & diagonal).astype(jnp.float32)
    )
    weight = own_block[:, 3, :, None, :, None] * far_block[:, 3, :, :, None, :]
    strength = block_count / (8.0 * partners)
    return (
        0.5 * strength * jnp.sum(weight * jnp.exp(-0.5 * squared) * kept_pairs, axis=(1, 2, 3, 4))
    )


def energy_of(extended, companion_group_indices, beside_all, iteration_number):
    lists_now = companion_group_indices[iteration_number]
    block_count = lists_now.shape[0]
    blocks = split_blocks(extended, block_count)
    per_walker = pair_terms(blocks, block_count, lists_now, jnp.ones(lists_now.shape, jnp.float32))
    total = jnp.sum(per_walker)
    return (total, per_walker)


def widen(layer):
    return with_halo(layer, (("atom", 2),), layer.shape[2])


def settle(gradient):
    block_width = gradient.shape[2] // 3
    padded = with_halo(gradient, (("atom", 2),), block_width)
    return (
        padded[:, :, 2 * block_width : 3 * block_width]
        + padded[:, :, :block_width]
        + padded[:, :, 4 * block_width :]
    )


def atom_total(partial_value):
    return lax.psum(partial_value, "atom")


def force_from(particle_location, interaction_strength, companion_group_indices, iteration_number):
    column = jnp.broadcast_to(
        interaction_strength[None, None, :],
        (particle_location.shape[0], 1, particle_location.shape[2]),
    )
    extended = widen(jnp.concatenate([particle_location, column], axis=1))
    (collapsed_total, per_walker), gradient = jax.value_and_grad(energy_of, has_aux=True)(
        extended, companion_group_indices, None, iteration_number
    )
    return (-settle(gradient[:, :3]), per_walker, extended)


def force_back(cot_force, extended, companion_group_indices, iteration_number):

    def slope_of(widened):
        return jax.grad(energy_of, has_aux=True)(
            widened, companion_group_indices, None, iteration_number
        )[0][:, :3]

    slope_now, pullback = jax.vjp(slope_of, extended)
    cot_extended = pullback(-widen(cot_force))[0]
    returned = settle(cot_extended)
    return (returned[:, :3], jnp.sum(returned[:, 3], axis=0))


def local_general(
    starting_locations,
    starting_speeds,
    terminal_location_adjoint,
    terminal_speed_adjoint,
    interaction_strength,
    reciprocal_particle_weight,
    heat_levels,
    swap_indicator,
    companion_group_indices,
):
    half_step = 0.5 * TIME_STEP
    atoms_all = starting_locations.shape[2] * lax.axis_size("atom")
    mass_row = reciprocal_particle_weight[None, None, :]
    steps_all = companion_group_indices.shape[0] - 1
    swap_at = steps_all // 2
    push_vectors, energy, extended = force_from(
        starting_locations, interaction_strength, companion_group_indices, 0
    )
    saved_extended = [extended]
    saved_updated = []
    saved_factor = []
    saved_current = []
    stored_goal = []
    particle_location, particle_speed = (starting_locations, starting_speeds)
    desired_heat_level = heat_levels
    partner_temp = from_partner(heat_levels, "rep", 0)
    upcoming_heat_level = jnp.where(swap_indicator == 1, partner_temp, heat_levels)
    interaction_multiplier = jnp.sqrt(upcoming_heat_level / heat_levels)[:, None, None]
    for iteration_number in range(steps_all):
        if iteration_number == swap_at:
            particle_speed = particle_speed * interaction_multiplier
            desired_heat_level = upcoming_heat_level
        mid_velocity = particle_speed + half_step * mass_row * push_vectors
        particle_location = particle_location + TIME_STEP * mid_velocity
        push_vectors, energy, extended = force_from(
            particle_location, interaction_strength, companion_group_indices, iteration_number + 1
        )
        updated = mid_velocity + half_step * mass_row * push_vectors
        kinetic, energy = atom_total(
            (0.5 * jnp.sum(updated * updated / mass_row, axis=(1, 2)), energy)
        )
        present_state = 2.0 * kinetic / (3 * atoms_all) + KINETIC_EPSILON
        rescaling_multiplier = jnp.sqrt(
            1.0 + THERMO_RELAX * (desired_heat_level / present_state - 1.0)
        )
        particle_speed = rescaling_multiplier[:, None, None] * updated
        saved_extended.append(extended)
        saved_updated.append(updated)
        saved_factor.append(rescaling_multiplier)
        saved_current.append(present_state)
        stored_goal.append(desired_heat_level)
    energies = energy / atoms_all
    cot_x, cot_v = (terminal_location_adjoint, terminal_speed_adjoint)
    cot_f = jnp.zeros_like(cot_x)
    cot_coupling = jnp.zeros_like(interaction_strength)
    for iteration_number in reversed(range(steps_all)):
        updated = saved_updated[iteration_number]
        rescaling_multiplier = saved_factor[iteration_number]
        present_state = saved_current[iteration_number]
        desired_heat_level = stored_goal[iteration_number]
        inner_sum = atom_total(jnp.sum(cot_v * updated, axis=(1, 2)))
        slope_factor = (
            -THERMO_RELAX
            * desired_heat_level
            / (present_state * present_state)
            * (2.0 / (3 * atoms_all))
            / (2.0 * rescaling_multiplier)
        )
        cot_updated = (
            rescaling_multiplier[:, None, None] * cot_v
            + (inner_sum * slope_factor)[:, None, None] * updated / mass_row
        )
        cot_force_now = cot_f + half_step * mass_row * cot_updated
        returned_x, returned_c = force_back(
            cot_force_now,
            saved_extended[iteration_number + 1],
            companion_group_indices,
            iteration_number + 1,
        )
        cot_coupling = cot_coupling + returned_c
        cot_x = cot_x + returned_x
        cot_mid = cot_updated + TIME_STEP * cot_x
        cot_v = cot_mid
        cot_f = half_step * mass_row * cot_mid
        if iteration_number == swap_at:
            cot_v = cot_v * interaction_multiplier
    returned_x, returned_c = force_back(cot_f, saved_extended[0], companion_group_indices, 0)
    cot_x = cot_x + returned_x
    cot_coupling = cot_coupling + returned_c
    grad_coupling = lax.psum(cot_coupling, "rep")
    return (particle_location, particle_speed, energies, cot_x, cot_v, grad_coupling)


LOG2E = math.log2(math.e)
ROWS = 16
KDIST = 32
KCROSS = 48
UNROLL = 4


def split3(x):
    hi = x.astype(jnp.bfloat16).astype(jnp.float32)
    rest = x - hi
    mid = rest.astype(jnp.bfloat16).astype(jnp.float32)
    low = (rest - mid).astype(jnp.bfloat16).astype(jnp.float32)
    return hi, mid, low


def row_sum(x):
    return jnp.sum(x, axis=1, keepdims=True)


def whole_sum(x):
    return jnp.full((1, x.shape[-1]), jnp.sum(x), jnp.float32)


def replica_kernel(
    far_ref,
    temp_ref,
    x0_ref,
    v0_ref,
    cx_ref,
    cv_ref,
    c_ref,
    m_ref,
    xf_ref,
    vf_ref,
    en_ref,
    gx_ref,
    gv_ref,
    gc_ref,
    left,
    right,
    left_w,
    right_w,
    rows_w,
    rows_x,
    rows_g,
    weights,
    acc_w,
    acc_v,
    out_w,
    out_v,
    saved_u,
    f_ref,
    fac_ref,
    cur_ref,
):
    owners, _, atoms = x0_ref.shape
    nb, _, width = f_ref.shape
    blocks = nb // owners
    evals = rows_x.shape[0]
    steps = evals - 1
    partners = 2
    half = 0.5 * TIME_STEP
    block_count = blocks
    dof = float(3 * nb * width)
    f32, bf16 = jnp.float32, jnp.bfloat16
    real = slice(0, nb)
    t_first = temp_ref[0:1]
    t_last = temp_ref[1:2]
    swap_gain = jnp.sqrt(t_last / t_first)
    strength = 0.5 * block_count / (8.0 * partners)
    log_scale = math.log2(strength)

    def whole(ref):
        return jnp.stack(
            [
                ref[o, :, j * width : (j + 1) * width]
                for o in range(owners)
                for j in range(blocks)
            ]
        )

    def give(ref, value):
        for o in range(owners):
            for j in range(blocks):
                ref[o, :, j * width : (j + 1) * width] = value[o * blocks + j]

    def far(n, p, k):
        return far_ref[p // blocks, (n * blocks + p % blocks) * partners + k]

    mass = whole(m_ref)
    coupling = whole(c_ref)

    for ref in (left_w, right_w, rows_w):
        ref[...] = jnp.zeros_like(ref)
    rows_x[...] = jnp.zeros_like(rows_x)
    rows_g[...] = jnp.zeros_like(rows_g)

    def put(ref, at, value):
        ref[real, at : at + value.shape[1], :] = value

    one = jnp.ones((nb, 1, width), f32)
    zero_pad = (((0,), (0,)), ((), ()))

    def pair(ref, n, p):
        return jnp.concatenate([ref[far(n, p, k)] for k in range(partners)], axis=1)

    def scatter(out, acc, n):
        for p in range(nb):
            for k in range(partners):
                q = far(n, p, k)
                acc[q] = acc[q] + out[p, :, k * width : (k + 1) * width]

    def set_rows(dest, value):
        hi, mid, low = split3(value)
        put(rows_w, 0, hi)
        put(rows_w, 3, mid)
        put(rows_w, 6, low)
        put(rows_w, 9, one)
        dest[...] = rows_w[...].astype(bf16)

    def products(first, second, at):
        for i, j in ((0, 0), (0, 1), (1, 0), (0, 2), (1, 1), (2, 0)):
            put(left_w, at, first[i])
            put(right_w, at, second[j])
            at += first[0].shape[1]
        return at

    def singles(ref, other, value, at):
        for part in split3(value):
            put(ref, at, part)
            put(other, at, one)
            at += 1
        return at

    def force(x, n):
        set_rows(rows_x.at[n], x)
        self_term = -0.5 * LOG2E * row_sum(x * x) + jnp.log(coupling) * LOG2E
        at = products(split3(x * LOG2E), split3(x), 0)
        at = singles(left_w, right_w, self_term + log_scale, at)
        at = singles(right_w, left_w, self_term, at)
        right_w[nb, at - 3 : at - 2, :] = jnp.full((1, width), -1e6, f32)
        left[:, 0:KDIST, :] = left_w[real, 0:KDIST, :].astype(bf16)
        right[:, 0:KDIST, :] = right_w[:, 0:KDIST, :].astype(bf16)

        @pl.loop(0, nb // UNROLL)
        def _(chunk):
            for i in range(UNROLL):
                p = chunk * UNROLL + i
                exponent = lax.dot_general(
                    left[p, 0:KDIST, :],
                    pair(right.at[:, 0:KDIST, :], n, p),
                    zero_pad,
                    preferred_element_type=f32,
                )
                w = jnp.exp2(exponent).astype(bf16)
                weights[n, p] = w
                out_w[p] = jnp.dot(rows_x[n, p], w, preferred_element_type=f32)
                acc_w[p] = lax.dot_general(
                    pair(rows_x.at[n], n, p),
                    w,
                    (((1,), (1,)), ((), ())),
                    preferred_element_type=f32,
                )

        scatter(out_w, acc_w, n)
        pulled = acc_w[real, 0:3, :] + acc_w[real, 3:6, :] + acc_w[real, 6:9, :]
        f_ref[...] = x * acc_w[real, 9:10, :] - pulled

    def force_back(g, n):
        x = (
            rows_x[n, real].astype(f32)[:, 0:3]
            + rows_x[n, real].astype(f32)[:, 3:6]
            + rows_x[n, real].astype(f32)[:, 6:9]
        )
        set_rows(rows_g, g)
        sx, sg = split3(x), split3(g)
        neg_g = tuple(-part for part in sg)
        neg_x = tuple(-part for part in sx)
        at = products(sx, neg_g, 0)
        at = products(sg, neg_x, at)
        own = row_sum(x * g)
        at = singles(left_w, right_w, own, at)
        singles(right_w, left_w, own, at)
        left[...] = left_w[real].astype(bf16)
        right[...] = right_w[...].astype(bf16)

        @pl.loop(0, nb // UNROLL)
        def _(chunk):
            for i in range(UNROLL):
                p = chunk * UNROLL + i
                phi = lax.dot_general(
                    left[p], pair(right, n, p), zero_pad, preferred_element_type=f32
                )
                w = weights[n, p]
                v = (w.astype(f32) * phi).astype(bf16)
                out_w[p] = jnp.dot(rows_g[p], w, preferred_element_type=f32)
                out_v[p] = jnp.dot(rows_x[n, p], v, preferred_element_type=f32)
                acc_w[p] = lax.dot_general(
                    pair(rows_g, n, p),
                    w,
                    (((1,), (1,)), ((), ())),
                    preferred_element_type=f32,
                )
                acc_v[p] = lax.dot_general(
                    pair(rows_x.at[n], n, p),
                    v,
                    (((1,), (1,)), ((), ())),
                    preferred_element_type=f32,
                )

        scatter(out_w, acc_w, n)
        scatter(out_v, acc_v, n)
        pulled_w = acc_w[real, 0:3, :] + acc_w[real, 3:6, :] + acc_w[real, 6:9, :]
        pulled_v = acc_v[real, 0:3, :] + acc_v[real, 3:6, :] + acc_v[real, 6:9, :]
        total_v = acc_v[real, 9:10, :]
        back_x = g * acc_w[real, 9:10, :] - pulled_w - x * total_v + pulled_v
        return back_x, total_v

    x, v, goal = whole(x0_ref), whole(v0_ref), t_first
    force(x, 0)
    for n in range(steps):
        if n == steps // 2:
            v = v * swap_gain
            goal = t_last
        mid = v + half * mass * f_ref[...]
        x = x + TIME_STEP * mid
        force(x, n + 1)
        u = mid + half * mass * f_ref[...]
        kinetic = 0.5 * whole_sum(u * u / mass)
        current = 2.0 * kinetic / dof + KINETIC_EPSILON
        factor = jnp.sqrt(1.0 + THERMO_RELAX * (goal / current - 1.0))
        v = factor * u
        saved_u[n] = u
        fac_ref[n] = factor
        cur_ref[n] = current
    give(xf_ref, x)
    give(vf_ref, v)
    selfs = jnp.zeros((1, width), f32)
    square = strength * jnp.sum(coupling * coupling, axis=1)
    for p in range(nb):
        for k in range(partners):
            hit = (far(steps, p, k) == p).astype(f32)
            selfs = selfs + hit * square[p : p + 1]
    total = whole_sum(acc_w[real, 9:10, :]) * 0.5 - whole_sum(selfs)
    en_ref[...] = total / float(nb * width)

    cot_x, cot_v = whole(cx_ref), whole(cv_ref)
    cot_f = jnp.zeros_like(cot_x)
    cot_c = jnp.zeros((nb, 1, width), f32)
    for n in reversed(range(steps)):
        goal = t_last if n >= steps // 2 else t_first
        u, factor, current = saved_u[n], fac_ref[n], cur_ref[n]
        inner = whole_sum(cot_v * u)
        slope = -THERMO_RELAX * goal / (current * current) * (2.0 / dof) / (2.0 * factor)
        cot_u = factor * cot_v + (inner * slope) * u / mass
        back_x, back_c = force_back(cot_f + half * mass * cot_u, n + 1)
        cot_c = cot_c + back_c
        cot_x = cot_x + back_x
        cot_mid = cot_u + TIME_STEP * cot_x
        cot_v = cot_mid
        cot_f = half * mass * cot_mid
        if n == steps // 2:
            cot_v = cot_v * swap_gain
    back_x, back_c = force_back(cot_f, 0)
    give(gx_ref, cot_x + back_x)
    give(gv_ref, cot_v)
    give(gc_ref, (cot_c + back_c) / coupling)


def run_replica(far, temps, x0, v0, cx, cv, coupling, mass, evals, blocks):
    owners, _, atoms = x0.shape
    nb, width = owners * blocks, atoms // blocks
    f32, bf16 = jnp.float32, jnp.bfloat16
    vec = jax.ShapeDtypeStruct((owners, 3, atoms), f32)
    vmem = pl.BlockSpec(memory_space=pltpu.VMEM)
    smem = pl.BlockSpec(memory_space=pltpu.SMEM)
    return pl.pallas_call(
        replica_kernel,
        out_shape=(
            vec,
            vec,
            jax.ShapeDtypeStruct((1, width), f32),
            vec,
            vec,
            jax.ShapeDtypeStruct((owners, 1, atoms), f32),
        ),
        in_specs=[smem] + [vmem] * 7,
        out_specs=[vmem] * 6,
        scratch_shapes=[
            pltpu.VMEM((nb, KCROSS, width), bf16),
            pltpu.VMEM((nb + 1, KCROSS, width), bf16),
            pltpu.VMEM((nb + 1, KCROSS, width), f32),
            pltpu.VMEM((nb + 1, KCROSS, width), f32),
            pltpu.VMEM((nb + 1, ROWS, width), f32),
            pltpu.VMEM((evals, nb + 1, ROWS, width), bf16),
            pltpu.VMEM((nb + 1, ROWS, width), bf16),
            pltpu.VMEM((evals, nb, width, 2 * width), bf16),
            pltpu.VMEM((nb + 1, ROWS, width), f32),
            pltpu.VMEM((nb + 1, ROWS, width), f32),
            pltpu.VMEM((nb, ROWS, 2 * width), f32),
            pltpu.VMEM((nb, ROWS, 2 * width), f32),
            pltpu.VMEM((evals - 1, nb, 3, width), f32),
            pltpu.VMEM((nb, 3, width), f32),
            pltpu.VMEM((evals - 1, 1, width), f32),
            pltpu.VMEM((evals - 1, 1, width), f32),
        ],
        compiler_params=pltpu.CompilerParams(vmem_limit_bytes=60 * 1024 * 1024),
    )(far, temps, x0, v0, cx, cv, coupling, mass)


MESH = pl.DeviceIdType.MESH


def greet(peers):
    barrier = pltpu.get_barrier_semaphore()
    for peer in peers:
        pl.semaphore_signal(barrier, inc=1, device_id=peer, device_id_type=MESH)
    pl.semaphore_wait(barrier, len(peers))


def others(axis):
    me, count = lax.axis_index(axis), lax.axis_size(axis)
    return [lax.rem(me + d, count) for d in range(1, count)]


def entry_kernel(blocks, partners, *refs):
    ins, outs = refs[:9], refs[9:17]
    heat_in, send_sem, recv_sem, heat_send, heat_recv = refs[17:]
    split, shared = ins[:4], ins[4:7]
    heat_ref, flag_ref = ins[7:]
    temp_ref = outs[7]
    me, owners = lax.axis_index("atom"), lax.axis_size("atom")
    rep = lax.axis_index("rep")
    partner = rep + 1 - 2 * lax.rem(rep, 2)
    peers = others("atom")
    twin = {"rep": partner, "atom": me}
    greet([{"rep": rep, "atom": peer} for peer in peers] + [twin])
    heat_copy = pltpu.make_async_remote_copy(
        src_ref=heat_ref,
        dst_ref=heat_in,
        send_sem=heat_send,
        recv_sem=heat_recv,
        device_id=twin,
        device_id_type=MESH,
    )
    heat_copy.start()
    copies = []
    for d, peer in enumerate(peers):
        for i in range(7):
            copies.append(
                pltpu.make_async_remote_copy(
                    src_ref=ins[i].at[peer] if i < 4 else ins[i],
                    dst_ref=outs[i].at[me],
                    send_sem=send_sem.at[d, i],
                    recv_sem=recv_sem.at[d, i],
                    device_id={"rep": rep, "atom": peer},
                    device_id_type=MESH,
                )
            )
            copies[-1].start()
    for i in range(7):
        outs[i][me] = ins[i][me] if i < 4 else ins[i][...]
    heat_copy.wait()
    own = heat_ref[...]
    upcoming = jnp.where(flag_ref[...] == 1, heat_in[...], own)
    lane = lax.broadcasted_iota(jnp.int32, own.shape, 1)
    for row, value in enumerate((own, upcoming)):
        chosen = jnp.sum(jnp.where(lane == me, value, 0.0), axis=1, keepdims=True)
        temp_ref[row : row + 1, :] = jnp.broadcast_to(chosen, own.shape)
    for copy in copies:
        copy.wait()
    slots = outs[6][...]
    owner = lax.broadcasted_iota(jnp.int32, slots.shape, 0)
    block = slots + (owner - 1) * blocks
    inside = (block >= 0) & (block < owners * blocks)
    outs[6][...] = jnp.where(inside, block, owners * blocks)


def exit_kernel(*refs):
    ins, outs = refs[:6], refs[6:12]
    en_in, gc_in, rep_in, total, send_sem, recv_sem, rep_send, rep_recv = refs[12:]
    en_ref, gc_ref = ins[4], ins[5]
    me, rep = lax.axis_index("atom"), lax.axis_index("rep")
    peers, rep_peers = others("atom"), others("rep")
    greet(
        [{"rep": rep, "atom": peer} for peer in peers]
        + [{"rep": peer, "atom": me} for peer in rep_peers]
    )
    dests = (gc_in,) + tuple(outs[:4]) + (en_in,)
    sources = (gc_ref,) + tuple(ins[:4]) + (en_ref,)
    copies = {}
    for i in range(6):
        for d, peer in enumerate(peers):
            copies[d, i] = pltpu.make_async_remote_copy(
                src_ref=sources[i].at[peer] if i < 5 else sources[i],
                dst_ref=dests[i].at[me] if i else gc_in.at[d],
                send_sem=send_sem.at[d, i],
                recv_sem=recv_sem.at[d, i],
                device_id={"rep": rep, "atom": peer},
                device_id_type=MESH,
            )
            copies[d, i].start()
    part = gc_ref[me]
    for d in range(len(peers)):
        copies[d, 0].wait()
        part = part + gc_in[d]
    total[...] = part
    rep_copies = []
    for d, peer in enumerate(rep_peers):
        rep_copies.append(
            pltpu.make_async_remote_copy(
                src_ref=total,
                dst_ref=rep_in.at[d],
                send_sem=rep_send.at[d],
                recv_sem=rep_recv.at[d],
                device_id={"rep": peer, "atom": me},
                device_id_type=MESH,
            )
        )
        rep_copies[-1].start()
    for i in range(4):
        outs[i][me] = ins[i][me]
    en_in[me] = en_ref[...]
    for d in range(len(peers)):
        for i in range(1, 6):
            copies[d, i].wait()
    outs[4][...] = en_in[...]
    for d, copy in enumerate(rep_copies):
        copy.wait()
        part = part + rep_in[d]
    outs[5][...] = part


def enter(split, shared, heat, flags, blocks, partners):
    f32 = jnp.float32
    owners = lax.axis_size("atom")
    vmem = pl.BlockSpec(memory_space=pltpu.VMEM)
    dma = pltpu.SemaphoreType.DMA
    return pl.pallas_call(
        functools.partial(entry_kernel, blocks, partners),
        out_shape=tuple(jax.ShapeDtypeStruct(a.shape, f32) for a in split)
        + tuple(jax.ShapeDtypeStruct((owners,) + a.shape, a.dtype) for a in shared)
        + (jax.ShapeDtypeStruct((2, heat.shape[1]), f32),),
        in_specs=[vmem] * 9,
        out_specs=[vmem] * 8,
        scratch_shapes=[
            pltpu.VMEM(heat.shape, f32),
            dma((owners - 1, 7)),
            dma((owners - 1, 7)),
            dma,
            dma,
        ],
        compiler_params=pltpu.CompilerParams(collective_id=0, has_side_effects=True),
    )(*split, *shared, heat, flags)


def leave(xf, vf, gx, gv, en, gc):
    f32 = jnp.float32
    owners, reps = lax.axis_size("atom"), lax.axis_size("rep")
    vmem = pl.BlockSpec(memory_space=pltpu.VMEM)
    dma = pltpu.SemaphoreType.DMA
    vec = jax.ShapeDtypeStruct(xf.shape, f32)
    return pl.pallas_call(
        exit_kernel,
        out_shape=(vec, vec, vec, vec)
        + (
            jax.ShapeDtypeStruct((owners,) + en.shape, f32),
            jax.ShapeDtypeStruct(gc.shape[1:], f32),
        ),
        in_specs=[vmem] * 6,
        out_specs=[vmem] * 6,
        scratch_shapes=[
            pltpu.VMEM((owners,) + en.shape, f32),
            pltpu.VMEM((owners - 1,) + gc.shape[1:], f32),
            pltpu.VMEM((reps - 1,) + gc.shape[1:], f32),
            pltpu.VMEM(gc.shape[1:], f32),
            dma((owners - 1, 6)),
            dma((owners - 1, 6)),
            dma((reps - 1,)),
            dma((reps - 1,)),
        ],
        compiler_params=pltpu.CompilerParams(collective_id=1, has_side_effects=True),
    )(xf, vf, gx, gv, en, gc)


def local_whole(
    starting_locations,
    starting_speeds,
    terminal_location_adjoint,
    terminal_speed_adjoint,
    interaction_strength,
    reciprocal_particle_weight,
    heat_levels,
    swap_indicator,
    companion_group_indices,
):
    evals, blocks, partners = companion_group_indices.shape
    lanes = starting_locations.shape[2] // blocks

    def row(x):
        x = x.reshape(1, -1)
        return jnp.pad(x, ((0, 0), (0, -x.shape[1] % lanes)))

    *mine, coupling, mass, far, temps = enter(
        (starting_locations, starting_speeds, terminal_location_adjoint, terminal_speed_adjoint),
        (row(interaction_strength), row(reciprocal_particle_weight), row(companion_group_indices)),
        row(heat_levels),
        row(swap_indicator),
        blocks,
        partners,
    )
    xf, vf, en, gx, gv, gc = run_replica(
        far[:, 0], temps, *mine, coupling, mass, evals, blocks
    )
    xf, vf, gx, gv, energies, grad_coupling = leave(xf, vf, gx, gv, en, gc)
    return (xf, vf, energies[:, 0, 0], gx, gv, grad_coupling.reshape(-1))


def local(*args):
    partners = args[8].shape[2]
    fits = args[0].shape[0] == lax.axis_size("atom") and partners == 2
    if fits and lax.axis_size("rep") % 2 == 0:
        return local_whole(*args)
    return local_general(*args)


def solution(mesh):
    in_specs = (
        P("rep", None, "atom"),
        P("rep", None, "atom"),
        P("rep", None, "atom"),
        P("rep", None, "atom"),
        P("atom"),
        P("atom"),
        P("rep"),
        P("rep"),
        P(None, "atom", None),
    )
    out_specs = (
        P("rep", None, "atom"),
        P("rep", None, "atom"),
        P("rep"),
        P("rep", None, "atom"),
        P("rep", None, "atom"),
        P("atom"),
    )
    return jax.shard_map(local, mesh=mesh, in_specs=in_specs, out_specs=out_specs, check_vma=False)
```

```python
import functools
import math

import jax
import jax.numpy as jnp
from jax import lax
from jax.experimental import pallas as pl
from jax.experimental.pallas import tpu as pltpu
from jax.sharding import PartitionSpec as P

TIME_STEP = 0.05
THERMO_RELAX = 0.5
KINETIC_EPSILON = 1e-06


def with_halo(block, sides, width):
    for axis, dim in sides:
        count = lax.axis_size(axis)
        forward = [(i, i + 1) for i in range(count - 1)]
        backward = [(target, source) for source, target in forward]
        low = lax.ppermute(
            lax.slice_in_dim(block, block.shape[dim] - width, None, axis=dim), axis, forward
        )
        high = lax.ppermute(lax.slice_in_dim(block, 0, width, axis=dim), axis, backward)
        block = jnp.concatenate([low, block, high], axis=dim)
    return block


def from_partner(x, axis, apart):
    return lax.ppermute(x, axis, [(i, i ^ 1 << apart) for i in range(lax.axis_size(axis))])


def split_blocks(extended, block_count):
    block_width = extended.shape[2] // (3 * block_count)
    return extended.reshape(extended.shape[0], 4, 3 * block_count, block_width)


def pair_terms(blocks, own_start, far_ids, keep):
    block_count = far_ids.shape[0]
    partners = far_ids.shape[1]
    block_width = blocks.shape[3]
    own_block = blocks[:, :, own_start : own_start + block_count]
    far_block = jnp.take(blocks, far_ids, axis=2)
    squared = jnp.zeros(
        (blocks.shape[0], block_count, partners, block_width, block_width), jnp.float32
    )
    for axis_id in range(3):
        offset = own_block[:, axis_id, :, None, :, None] - far_block[:, axis_id, :, :, None, :]
        squared = squared + offset * offset
    own_ids = own_start + jnp.arange(block_count, dtype=jnp.int32)
    self_block = far_ids == own_ids[:, None]
    diagonal = jnp.arange(block_width)[:, None] == jnp.arange(block_width)[None, :]
    kept_pairs = keep[:, :, None, None] * (
        1.0 - (self_block[:, :, None, None] & diagonal).astype(jnp.float32)
    )
    weight = own_block[:, 3, :, None, :, None] * far_block[:, 3, :, :, None, :]
    strength = block_count / (8.0 * partners)
    return (
        0.5 * strength * jnp.sum(weight * jnp.exp(-0.5 * squared) * kept_pairs, axis=(1, 2, 3, 4))
    )


def energy_of(extended, companion_group_indices, beside_all, iteration_number):
    lists_now = companion_group_indices[iteration_number]
    block_count = lists_now.shape[0]
    blocks = split_blocks(extended, block_count)
    per_walker = pair_terms(blocks, block_count, lists_now, jnp.ones(lists_now.shape, jnp.float32))
    total = jnp.sum(per_walker)
    return (total, per_walker)


def widen(layer):
    return with_halo(layer, (("atom", 2),), layer.shape[2])


def settle(gradient):
    block_width = gradient.shape[2] // 3
    padded = with_halo(gradient, (("atom", 2),), block_width)
    return (
        padded[:, :, 2 * block_width : 3 * block_width]
        + padded[:, :, :block_width]
        + padded[:, :, 4 * block_width :]
    )


def atom_total(partial_value):
    return lax.psum(partial_value, "atom")


def force_from(particle_location, interaction_strength, companion_group_indices, iteration_number):
    column = jnp.broadcast_to(
        interaction_strength[None, None, :],
        (particle_location.shape[0], 1, particle_location.shape[2]),
    )
    extended = widen(jnp.concatenate([particle_location, column], axis=1))
    (collapsed_total, per_walker), gradient = jax.value_and_grad(energy_of, has_aux=True)(
        extended, companion_group_indices, None, iteration_number
    )
    return (-settle(gradient[:, :3]), per_walker, extended)


def force_back(cot_force, extended, companion_group_indices, iteration_number):

    def slope_of(widened):
        return jax.grad(energy_of, has_aux=True)(
            widened, companion_group_indices, None, iteration_number
        )[0][:, :3]

    slope_now, pullback = jax.vjp(slope_of, extended)
    cot_extended = pullback(-widen(cot_force))[0]
    returned = settle(cot_extended)
    return (returned[:, :3], jnp.sum(returned[:, 3], axis=0))


def local_general(
    starting_locations,
    starting_speeds,
    terminal_location_adjoint,
    terminal_speed_adjoint,
    interaction_strength,
    reciprocal_particle_weight,
    heat_levels,
    swap_indicator,
    companion_group_indices,
):
    half_step = 0.5 * TIME_STEP
    atoms_all = starting_locations.shape[2] * lax.axis_size("atom")
    mass_row = reciprocal_particle_weight[None, None, :]
    steps_all = companion_group_indices.shape[0] - 1
    swap_at = steps_all // 2
    push_vectors, energy, extended = force_from(
        starting_locations, interaction_strength, companion_group_indices, 0
    )
    saved_extended = [extended]
    saved_updated = []
    saved_factor = []
    saved_current = []
    stored_goal = []
    particle_location, particle_speed = (starting_locations, starting_speeds)
    desired_heat_level = heat_levels
    partner_temp = from_partner(heat_levels, "rep", 0)
    upcoming_heat_level = jnp.where(swap_indicator == 1, partner_temp, heat_levels)
    interaction_multiplier = jnp.sqrt(upcoming_heat_level / heat_levels)[:, None, None]
    for iteration_number in range(steps_all):
        if iteration_number == swap_at:
            particle_speed = particle_speed * interaction_multiplier
            desired_heat_level = upcoming_heat_level
        mid_velocity = particle_speed + half_step * mass_row * push_vectors
        particle_location = particle_location + TIME_STEP * mid_velocity
        push_vectors, energy, extended = force_from(
            particle_location, interaction_strength, companion_group_indices, iteration_number + 1
        )
        updated = mid_velocity + half_step * mass_row * push_vectors
        kinetic, energy = atom_total(
            (0.5 * jnp.sum(updated * updated / mass_row, axis=(1, 2)), energy)
        )
        present_state = 2.0 * kinetic / (3 * atoms_all) + KINETIC_EPSILON
        rescaling_multiplier = jnp.sqrt(
            1.0 + THERMO_RELAX * (desired_heat_level / present_state - 1.0)
        )
        particle_speed = rescaling_multiplier[:, None, None] * updated
        saved_extended.append(extended)
        saved_updated.append(updated)
        saved_factor.append(rescaling_multiplier)
        saved_current.append(present_state)
        stored_goal.append(desired_heat_level)
    energies = energy / atoms_all
    cot_x, cot_v = (terminal_location_adjoint, terminal_speed_adjoint)
    cot_f = jnp.zeros_like(cot_x)
    cot_coupling = jnp.zeros_like(interaction_strength)
    for iteration_number in reversed(range(steps_all)):
        updated = saved_updated[iteration_number]
        rescaling_multiplier = saved_factor[iteration_number]
        present_state = saved_current[iteration_number]
        desired_heat_level = stored_goal[iteration_number]
        inner_sum = atom_total(jnp.sum(cot_v * updated, axis=(1, 2)))
        slope_factor = (
            -THERMO_RELAX
            * desired_heat_level
            / (present_state * present_state)
            * (2.0 / (3 * atoms_all))
            / (2.0 * rescaling_multiplier)
        )
        cot_updated = (
            rescaling_multiplier[:, None, None] * cot_v
            + (inner_sum * slope_factor)[:, None, None] * updated / mass_row
        )
        cot_force_now = cot_f + half_step * mass_row * cot_updated
        returned_x, returned_c = force_back(
            cot_force_now,
            saved_extended[iteration_number + 1],
            companion_group_indices,
            iteration_number + 1,
        )
        cot_coupling = cot_coupling + returned_c
        cot_x = cot_x + returned_x
        cot_mid = cot_updated + TIME_STEP * cot_x
        cot_v = cot_mid
        cot_f = half_step * mass_row * cot_mid
        if iteration_number == swap_at:
            cot_v = cot_v * interaction_multiplier
    returned_x, returned_c = force_back(cot_f, saved_extended[0], companion_group_indices, 0)
    cot_x = cot_x + returned_x
    cot_coupling = cot_coupling + returned_c
    grad_coupling = lax.psum(cot_coupling, "rep")
    return (particle_location, particle_speed, energies, cot_x, cot_v, grad_coupling)


LOG2E = math.log2(math.e)
ROWS = 16
KDIST = 16
KCROSS = 32
KEPT = 8
UNROLL = 8


def split2(x):
    hi = x.astype(jnp.bfloat16).astype(jnp.float32)
    return hi, (x - hi).astype(jnp.bfloat16).astype(jnp.float32)


def row_sum(x):
    return jnp.sum(x, axis=1, keepdims=True)


def whole_sum(x):
    return jnp.full((1, x.shape[-1]), jnp.sum(x), jnp.float32)


def replica_kernel(
    far_ref,
    temp_ref,
    x0_ref,
    v0_ref,
    cx_ref,
    cv_ref,
    c_ref,
    m_ref,
    xf_ref,
    vf_ref,
    en_ref,
    gx_ref,
    gv_ref,
    gc_ref,
    left,
    right,
    left_w,
    right_w,
    rows_w,
    rows_x,
    rows_g,
    weights,
    acc_w,
    acc_v,
    out_w,
    out_v,
    saved_u,
    saved_x,
    f_ref,
    fac_ref,
    cur_ref,
):
    owners, _, atoms = x0_ref.shape
    nb, _, width = f_ref.shape
    blocks = nb // owners
    evals = rows_x.shape[0]
    steps = evals - 1
    partners = 2
    half = 0.5 * TIME_STEP
    block_count = blocks
    dof = float(3 * nb * width)
    f32, bf16 = jnp.float32, jnp.bfloat16
    real = slice(0, nb)
    t_first = temp_ref[0:1]
    t_last = temp_ref[1:2]
    swap_gain = jnp.sqrt(t_last / t_first)
    strength = 0.5 * block_count / (8.0 * partners)
    log_scale = math.log2(strength)

    def whole(ref):
        return jnp.stack(
            [
                ref[o, :, j * width : (j + 1) * width]
                for o in range(owners)
                for j in range(blocks)
            ]
        )

    def give(ref, value):
        for o in range(owners):
            for j in range(blocks):
                ref[o, :, j * width : (j + 1) * width] = value[o * blocks + j]

    def far(n, p, k):
        return far_ref[p // blocks, n, k, p % blocks]

    mass = whole(m_ref)
    coupling = whole(c_ref)

    for ref in (left_w, right_w, rows_w):
        ref[...] = jnp.zeros_like(ref)
    rows_x[...] = jnp.zeros_like(rows_x)
    rows_g[...] = jnp.zeros_like(rows_g)

    def put(ref, at, value):
        ref[real, at : at + value.shape[1], :] = value

    one = jnp.ones((nb, 1, width), f32)
    zero_pad = (((0,), (0,)), ((), ()))

    def pair(ref, n, p):
        return jnp.concatenate([ref[far(n, p, k)] for k in range(partners)], axis=1)

    def scatter(out, acc, n):
        for p in range(nb):
            for k in range(partners):
                q = far(n, p, k)
                acc[q] = acc[q] + out[p, :, k * width : (k + 1) * width]

    def set_rows(dest, value):
        hi, low = split2(value)
        put(rows_w, 0, hi)
        put(rows_w, 3, low)
        put(rows_w, 6, one)
        dest[...] = rows_w[...].astype(bf16)

    def products(first, second, at):
        for i, j in ((0, 0), (0, 1), (1, 0)):
            put(left_w, at, first[i])
            put(right_w, at, second[j])
            at += first[0].shape[1]
        return at

    def singles(ref, other, value, at):
        for part in split2(value):
            put(ref, at, part)
            put(other, at, one)
            at += 1
        return at

    def force(x, n):
        set_rows(rows_x.at[n], x)
        saved_x[n] = x
        self_term = -0.5 * LOG2E * row_sum(x * x) + jnp.log(coupling) * LOG2E
        at = products(split2(x * LOG2E), split2(x), 0)
        at = singles(left_w, right_w, self_term + log_scale, at)
        at = singles(right_w, left_w, self_term, at)
        right_w[nb, at - 2 : at - 1, :] = jnp.full((1, width), -1e6, f32)
        left[:, 0:KDIST, :] = left_w[real, 0:KDIST, :].astype(bf16)
        right[:, 0:KDIST, :] = right_w[:, 0:KDIST, :].astype(bf16)

        @pl.loop(0, nb // UNROLL)
        def _(chunk):
            for i in range(UNROLL):
                p = chunk * UNROLL + i
                exponent = lax.dot_general(
                    left[p, 0:KDIST, :],
                    pair(right.at[:, 0:KDIST, :], n, p),
                    zero_pad,
                    preferred_element_type=f32,
                )
                w = jnp.exp2(exponent).astype(bf16)
                weights[n, p] = w
                out_w[p] = jnp.dot(rows_x[n, p], w, preferred_element_type=f32)[:KEPT]
                acc_w[p] = lax.dot_general(
                    pair(rows_x.at[n], n, p),
                    w,
                    (((1,), (1,)), ((), ())),
                    preferred_element_type=f32,
                )[:KEPT]

        scatter(out_w, acc_w, n)
        pulled = acc_w[real, 0:3, :] + acc_w[real, 3:6, :]
        f_ref[...] = x * acc_w[real, 6:7, :] - pulled

    def force_back(g, n):
        x = saved_x[n]
        set_rows(rows_g, g)
        sx, sg = split2(x), split2(g)
        neg_g = tuple(-part for part in sg)
        neg_x = tuple(-part for part in sx)
        at = products(sx, neg_g, 0)
        at = products(sg, neg_x, at)
        own = row_sum(x * g)
        at = singles(left_w, right_w, own, at)
        singles(right_w, left_w, own, at)
        left[...] = left_w[real].astype(bf16)
        right[...] = right_w[...].astype(bf16)

        @pl.loop(0, nb // UNROLL)
        def _(chunk):
            for i in range(UNROLL):
                p = chunk * UNROLL + i
                phi = lax.dot_general(
                    left[p], pair(right, n, p), zero_pad, preferred_element_type=f32
                )
                w = weights[n, p]
                v = (w.astype(f32) * phi).astype(bf16)
                out_w[p] = jnp.dot(rows_g[p], w, preferred_element_type=f32)[:KEPT]
                out_v[p] = jnp.dot(rows_x[n, p], v, preferred_element_type=f32)[:KEPT]
                acc_w[p] = lax.dot_general(
                    pair(rows_g, n, p),
                    w,
                    (((1,), (1,)), ((), ())),
                    preferred_element_type=f32,
                )[:KEPT]
                acc_v[p] = lax.dot_general(
                    pair(rows_x.at[n], n, p),
                    v,
                    (((1,), (1,)), ((), ())),
                    preferred_element_type=f32,
                )[:KEPT]

        scatter(out_w, acc_w, n)
        scatter(out_v, acc_v, n)
        pulled_w = acc_w[real, 0:3, :] + acc_w[real, 3:6, :]
        pulled_v = acc_v[real, 0:3, :] + acc_v[real, 3:6, :]
        total_v = acc_v[real, 6:7, :]
        back_x = g * acc_w[real, 6:7, :] - pulled_w - x * total_v + pulled_v
        return back_x, total_v

    x, v, goal = whole(x0_ref), whole(v0_ref), t_first
    force(x, 0)
    for n in range(steps):
        if n == steps // 2:
            v = v * swap_gain
            goal = t_last
        mid = v + half * mass * f_ref[...]
        x = x + TIME_STEP * mid
        force(x, n + 1)
        u = mid + half * mass * f_ref[...]
        kinetic = 0.5 * whole_sum(u * u / mass)
        current = 2.0 * kinetic / dof + KINETIC_EPSILON
        factor = jnp.sqrt(1.0 + THERMO_RELAX * (goal / current - 1.0))
        v = factor * u
        saved_u[n] = u
        fac_ref[n] = factor
        cur_ref[n] = current
    give(xf_ref, x)
    give(vf_ref, v)
    selfs = jnp.zeros((1, width), f32)
    square = strength * jnp.sum(coupling * coupling, axis=1)
    for p in range(nb):
        for k in range(partners):
            hit = (far(steps, p, k) == p).astype(f32)
            selfs = selfs + hit * square[p : p + 1]
    total = whole_sum(acc_w[real, 6:7, :]) * 0.5 - whole_sum(selfs)
    en_ref[...] = total / float(nb * width)

    cot_x, cot_v = whole(cx_ref), whole(cv_ref)
    cot_f = jnp.zeros_like(cot_x)
    cot_c = jnp.zeros((nb, 1, width), f32)
    for n in reversed(range(steps)):
        goal = t_last if n >= steps // 2 else t_first
        u, factor, current = saved_u[n], fac_ref[n], cur_ref[n]
        inner = whole_sum(cot_v * u)
        slope = -THERMO_RELAX * goal / (current * current) * (2.0 / dof) / (2.0 * factor)
        cot_u = factor * cot_v + (inner * slope) * u / mass
        back_x, back_c = force_back(cot_f + half * mass * cot_u, n + 1)
        cot_c = cot_c + back_c
        cot_x = cot_x + back_x
        cot_mid = cot_u + TIME_STEP * cot_x
        cot_v = cot_mid
        cot_f = half * mass * cot_mid
        if n == steps // 2:
            cot_v = cot_v * swap_gain
    back_x, back_c = force_back(cot_f, 0)
    give(gx_ref, cot_x + back_x)
    give(gv_ref, cot_v)
    give(gc_ref, (cot_c + back_c) / coupling)


def run_replica(far, temps, x0, v0, cx, cv, coupling, mass, evals, blocks):
    owners, _, atoms = x0.shape
    nb, width = owners * blocks, atoms // blocks
    f32, bf16 = jnp.float32, jnp.bfloat16
    vec = jax.ShapeDtypeStruct((owners, 3, atoms), f32)
    vmem = pl.BlockSpec(memory_space=pltpu.VMEM)
    smem = pl.BlockSpec(memory_space=pltpu.SMEM)
    return pl.pallas_call(
        replica_kernel,
        out_shape=(
            vec,
            vec,
            jax.ShapeDtypeStruct((1, width), f32),
            vec,
            vec,
            jax.ShapeDtypeStruct((owners, 1, atoms), f32),
        ),
        in_specs=[smem] + [vmem] * 7,
        out_specs=[vmem] * 6,
        scratch_shapes=[
            pltpu.VMEM((nb, KCROSS, width), bf16),
            pltpu.VMEM((nb + 1, KCROSS, width), bf16),
            pltpu.VMEM((nb + 1, KCROSS, width), f32),
            pltpu.VMEM((nb + 1, KCROSS, width), f32),
            pltpu.VMEM((nb + 1, ROWS, width), f32),
            pltpu.VMEM((evals, nb + 1, ROWS, width), bf16),
            pltpu.VMEM((nb + 1, ROWS, width), bf16),
            pltpu.VMEM((evals, nb, width, 2 * width), bf16),
            pltpu.VMEM((nb + 1, KEPT, width), f32),
            pltpu.VMEM((nb + 1, KEPT, width), f32),
            pltpu.VMEM((nb, KEPT, 2 * width), f32),
            pltpu.VMEM((nb, KEPT, 2 * width), f32),
            pltpu.VMEM((evals - 1, nb, 3, width), f32),
            pltpu.VMEM((evals, nb, 3, width), f32),
            pltpu.VMEM((nb, 3, width), f32),
            pltpu.VMEM((evals - 1, 1, width), f32),
            pltpu.VMEM((evals - 1, 1, width), f32),
        ],
        compiler_params=pltpu.CompilerParams(vmem_limit_bytes=60 * 1024 * 1024),
    )(far, temps, x0, v0, cx, cv, coupling, mass)


MESH = pl.DeviceIdType.MESH


def greet(peers):
    barrier = pltpu.get_barrier_semaphore()
    for peer in peers:
        pl.semaphore_signal(barrier, inc=1, device_id=peer, device_id_type=MESH)
    pl.semaphore_wait(barrier, len(peers))


def others(axis):
    me, count = lax.axis_index(axis), lax.axis_size(axis)
    return [lax.rem(me + d, count) for d in range(1, count)]


def entry_kernel(blocks, partners, *refs):
    ins, outs = refs[:9], refs[9:17]
    stage = refs[17:21]
    heat_in, send_sem, recv_sem, heat_send, heat_recv = refs[21:]
    heat_ref, flag_ref = ins[7:]
    temp_ref = outs[7]
    me, owners = lax.axis_index("atom"), lax.axis_size("atom")
    rep = lax.axis_index("rep")
    partner = rep + 1 - 2 * lax.rem(rep, 2)
    peers = others("atom")
    for i in range(4):
        for r in range(owners):
            stage[i][r] = ins[i][:, r, :]
    twin = {"rep": partner, "atom": me}
    greet([{"rep": rep, "atom": peer} for peer in peers] + [twin])
    heat_copy = pltpu.make_async_remote_copy(
        src_ref=heat_ref,
        dst_ref=heat_in,
        send_sem=heat_send,
        recv_sem=heat_recv,
        device_id=twin,
        device_id_type=MESH,
    )
    heat_copy.start()
    copies = []
    for d, peer in enumerate(peers):
        for i in range(7):
            copies.append(
                pltpu.make_async_remote_copy(
                    src_ref=stage[i].at[peer] if i < 4 else ins[i],
                    dst_ref=outs[i].at[me],
                    send_sem=send_sem.at[d, i],
                    recv_sem=recv_sem.at[d, i],
                    device_id={"rep": rep, "atom": peer},
                    device_id_type=MESH,
                )
            )
            copies[-1].start()
    for i in range(7):
        outs[i][me] = stage[i][me] if i < 4 else ins[i][...]
    heat_copy.wait()
    own = heat_ref[...]
    upcoming = jnp.where(flag_ref[...] == 1, heat_in[...], own)
    lane = lax.broadcasted_iota(jnp.int32, own.shape, 1)
    for row, value in enumerate((own, upcoming)):
        chosen = jnp.sum(jnp.where(lane == me, value, 0.0), axis=1, keepdims=True)
        temp_ref[row : row + 1, :] = jnp.broadcast_to(chosen, (1, temp_ref.shape[1]))
    for copy in copies:
        copy.wait()
    slots = outs[6][...]
    owner = lax.broadcasted_iota(jnp.int32, slots.shape, 0)
    block = slots + (owner - 1) * blocks
    inside = (block >= 0) & (block < owners * blocks)
    outs[6][...] = jnp.where(inside, block, owners * blocks)


def exit_kernel(*refs):
    ins, outs = refs[:6], refs[6:12]
    land = refs[12:16]
    en_in, gc_in, rep_in, total, send_sem, recv_sem, rep_send, rep_recv = refs[16:]
    en_ref, gc_ref = ins[4], ins[5]
    me, rep = lax.axis_index("atom"), lax.axis_index("rep")
    peers, rep_peers = others("atom"), others("rep")
    greet(
        [{"rep": rep, "atom": peer} for peer in peers]
        + [{"rep": peer, "atom": me} for peer in rep_peers]
    )
    dests = (gc_in,) + tuple(land) + (en_in,)
    sources = (gc_ref,) + tuple(ins[:4]) + (en_ref,)
    copies = {}
    for i in range(6):
        for d, peer in enumerate(peers):
            copies[d, i] = pltpu.make_async_remote_copy(
                src_ref=sources[i].at[peer] if i < 5 else sources[i],
                dst_ref=dests[i].at[me] if i else gc_in.at[d],
                send_sem=send_sem.at[d, i],
                recv_sem=recv_sem.at[d, i],
                device_id={"rep": rep, "atom": peer},
                device_id_type=MESH,
            )
            copies[d, i].start()
    part = gc_ref[me]
    for d in range(len(peers)):
        copies[d, 0].wait()
        part = part + gc_in[d]
    total[...] = part
    rep_copies = []
    for d, peer in enumerate(rep_peers):
        rep_copies.append(
            pltpu.make_async_remote_copy(
                src_ref=total,
                dst_ref=rep_in.at[d],
                send_sem=rep_send.at[d],
                recv_sem=rep_recv.at[d],
                device_id={"rep": peer, "atom": me},
                device_id_type=MESH,
            )
        )
        rep_copies[-1].start()
    for i in range(4):
        land[i][me] = ins[i][me]
    en_in[me] = en_ref[...]
    for d in range(len(peers)):
        for i in range(1, 6):
            copies[d, i].wait()
    for i in range(4):
        for r in range(lax.axis_size("atom")):
            outs[i][:, r, :] = land[i][r]
    lane = lax.broadcasted_iota(jnp.int32, en_ref.shape, 1)
    energies = jnp.zeros(en_ref.shape, jnp.float32)
    for r in range(lax.axis_size("atom")):
        energies = jnp.where(lane == r, en_in[r], energies)
    outs[4][...] = energies[:, : outs[4].shape[1]]
    for d, copy in enumerate(rep_copies):
        copy.wait()
        part = part + rep_in[d]
    outs[5][...] = part


def enter(split, shared, heat, flags, blocks, partners, lanes):
    f32 = jnp.float32
    moved = [(a.shape[1], a.shape[0], a.shape[2]) for a in split]
    owners = lax.axis_size("atom")
    vmem = pl.BlockSpec(memory_space=pltpu.VMEM)
    dma = pltpu.SemaphoreType.DMA
    return pl.pallas_call(
        functools.partial(entry_kernel, blocks, partners),
        out_shape=tuple(jax.ShapeDtypeStruct(s, f32) for s in moved)
        + tuple(jax.ShapeDtypeStruct((owners,) + a.shape, a.dtype) for a in shared)
        + (jax.ShapeDtypeStruct((2, lanes), f32),),
        in_specs=[vmem] * 9,
        out_specs=[vmem] * 8,
        scratch_shapes=[pltpu.VMEM(s, f32) for s in moved]
        + [
            pltpu.VMEM(heat.shape, f32),
            dma((owners - 1, 7)),
            dma((owners - 1, 7)),
            dma,
            dma,
        ],
        compiler_params=pltpu.CompilerParams(collective_id=0, has_side_effects=True),
    )(*split, *shared, heat, flags)


def leave(xf, vf, gx, gv, en, gc):
    f32 = jnp.float32
    owners, reps = lax.axis_size("atom"), lax.axis_size("rep")
    vmem = pl.BlockSpec(memory_space=pltpu.VMEM)
    dma = pltpu.SemaphoreType.DMA
    vec = jax.ShapeDtypeStruct((xf.shape[1], owners, xf.shape[2]), f32)
    return pl.pallas_call(
        exit_kernel,
        out_shape=(vec, vec, vec, vec)
        + (
            jax.ShapeDtypeStruct((1, owners), f32),
            jax.ShapeDtypeStruct(gc.shape[1:], f32),
        ),
        in_specs=[vmem] * 6,
        out_specs=[vmem] * 6,
        scratch_shapes=[pltpu.VMEM(xf.shape, f32)] * 4
        + [
            pltpu.VMEM((owners,) + en.shape, f32),
            pltpu.VMEM((owners - 1,) + gc.shape[1:], f32),
            pltpu.VMEM((reps - 1,) + gc.shape[1:], f32),
            pltpu.VMEM(gc.shape[1:], f32),
            dma((owners - 1, 6)),
            dma((owners - 1, 6)),
            dma((reps - 1,)),
            dma((reps - 1,)),
        ],
        compiler_params=pltpu.CompilerParams(collective_id=1, has_side_effects=True),
    )(xf, vf, gx, gv, en, gc)


def local_whole(
    starting_locations,
    starting_speeds,
    terminal_location_adjoint,
    terminal_speed_adjoint,
    interaction_strength,
    reciprocal_particle_weight,
    heat_levels,
    swap_indicator,
    companion_group_indices,
):
    evals, blocks, partners = companion_group_indices.shape
    lanes = starting_locations.shape[2] // blocks

    def turned(x):
        return x.transpose(1, 0, 2)

    *mine, coupling, mass, far, temps = enter(
        tuple(
            turned(x)
            for x in (
                starting_locations,
                starting_speeds,
                terminal_location_adjoint,
                terminal_speed_adjoint,
            )
        ),
        (
            interaction_strength.reshape(1, -1),
            reciprocal_particle_weight.reshape(1, -1),
            companion_group_indices.transpose(0, 2, 1),
        ),
        heat_levels.reshape(1, -1),
        swap_indicator.reshape(1, -1),
        blocks,
        partners,
        lanes,
    )
    xf, vf, en, gx, gv, gc = run_replica(
        far, temps, *mine, coupling, mass, evals, blocks
    )
    xf, vf, gx, gv, energies, grad_coupling = leave(xf, vf, gx, gv, en, gc)
    return (
        turned(xf),
        turned(vf),
        energies[0],
        turned(gx),
        turned(gv),
        grad_coupling.reshape(-1),
    )


def local(*args):
    partners = args[8].shape[2]
    fits = args[0].shape[0] == lax.axis_size("atom") and partners == 2
    if fits and lax.axis_size("rep") % 2 == 0:
        return local_whole(*args)
    return local_general(*args)


def solution(mesh):
    in_specs = (
        P("rep", None, "atom"),
        P("rep", None, "atom"),
        P("rep", None, "atom"),
        P("rep", None, "atom"),
        P("atom"),
        P("atom"),
        P("rep"),
        P("rep"),
        P(None, "atom", None),
    )
    out_specs = (
        P("rep", None, "atom"),
        P("rep", None, "atom"),
        P("rep"),
        P("rep", None, "atom"),
        P("rep", None, "atom"),
        P("atom"),
    )
    return jax.shard_map(local, mesh=mesh, in_specs=in_specs, out_specs=out_specs, check_vma=False)
```

```python
import functools
import math

import jax
import jax.numpy as jnp
from jax import lax
from jax.experimental import pallas as pl
from jax.experimental.pallas import tpu as pltpu
from jax.sharding import PartitionSpec as P

TIME_STEP = 0.05
THERMO_RELAX = 0.5
KINETIC_EPSILON = 1e-06


def with_halo(block, sides, width):
    for axis, dim in sides:
        count = lax.axis_size(axis)
        forward = [(i, i + 1) for i in range(count - 1)]
        backward = [(target, source) for source, target in forward]
        low = lax.ppermute(
            lax.slice_in_dim(block, block.shape[dim] - width, None, axis=dim), axis, forward
        )
        high = lax.ppermute(lax.slice_in_dim(block, 0, width, axis=dim), axis, backward)
        block = jnp.concatenate([low, block, high], axis=dim)
    return block


def from_partner(x, axis, apart):
    return lax.ppermute(x, axis, [(i, i ^ 1 << apart) for i in range(lax.axis_size(axis))])


def split_blocks(extended, block_count):
    block_width = extended.shape[2] // (3 * block_count)
    return extended.reshape(extended.shape[0], 4, 3 * block_count, block_width)


def pair_terms(blocks, own_start, far_ids, keep):
    block_count = far_ids.shape[0]
    partners = far_ids.shape[1]
    block_width = blocks.shape[3]
    own_block = blocks[:, :, own_start : own_start + block_count]
    far_block = jnp.take(blocks, far_ids, axis=2)
    squared = jnp.zeros(
        (blocks.shape[0], block_count, partners, block_width, block_width), jnp.float32
    )
    for axis_id in range(3):
        offset = own_block[:, axis_id, :, None, :, None] - far_block[:, axis_id, :, :, None, :]
        squared = squared + offset * offset
    own_ids = own_start + jnp.arange(block_count, dtype=jnp.int32)
    self_block = far_ids == own_ids[:, None]
    diagonal = jnp.arange(block_width)[:, None] == jnp.arange(block_width)[None, :]
    kept_pairs = keep[:, :, None, None] * (
        1.0 - (self_block[:, :, None, None] & diagonal).astype(jnp.float32)
    )
    weight = own_block[:, 3, :, None, :, None] * far_block[:, 3, :, :, None, :]
    strength = block_count / (8.0 * partners)
    return (
        0.5 * strength * jnp.sum(weight * jnp.exp(-0.5 * squared) * kept_pairs, axis=(1, 2, 3, 4))
    )


def energy_of(extended, companion_group_indices, beside_all, iteration_number):
    lists_now = companion_group_indices[iteration_number]
    block_count = lists_now.shape[0]
    blocks = split_blocks(extended, block_count)
    per_walker = pair_terms(blocks, block_count, lists_now, jnp.ones(lists_now.shape, jnp.float32))
    total = jnp.sum(per_walker)
    return (total, per_walker)


def widen(layer):
    return with_halo(layer, (("atom", 2),), layer.shape[2])


def settle(gradient):
    block_width = gradient.shape[2] // 3
    padded = with_halo(gradient, (("atom", 2),), block_width)
    return (
        padded[:, :, 2 * block_width : 3 * block_width]
        + padded[:, :, :block_width]
        + padded[:, :, 4 * block_width :]
    )


def atom_total(partial_value):
    return lax.psum(partial_value, "atom")


def force_from(particle_location, interaction_strength, companion_group_indices, iteration_number):
    column = jnp.broadcast_to(
        interaction_strength[None, None, :],
        (particle_location.shape[0], 1, particle_location.shape[2]),
    )
    extended = widen(jnp.concatenate([particle_location, column], axis=1))
    (collapsed_total, per_walker), gradient = jax.value_and_grad(energy_of, has_aux=True)(
        extended, companion_group_indices, None, iteration_number
    )
    return (-settle(gradient[:, :3]), per_walker, extended)


def force_back(cot_force, extended, companion_group_indices, iteration_number):

    def slope_of(widened):
        return jax.grad(energy_of, has_aux=True)(
            widened, companion_group_indices, None, iteration_number
        )[0][:, :3]

    slope_now, pullback = jax.vjp(slope_of, extended)
    cot_extended = pullback(-widen(cot_force))[0]
    returned = settle(cot_extended)
    return (returned[:, :3], jnp.sum(returned[:, 3], axis=0))


def local_general(
    starting_locations,
    starting_speeds,
    terminal_location_adjoint,
    terminal_speed_adjoint,
    interaction_strength,
    reciprocal_particle_weight,
    heat_levels,
    swap_indicator,
    companion_group_indices,
):
    half_step = 0.5 * TIME_STEP
    atoms_all = starting_locations.shape[2] * lax.axis_size("atom")
    mass_row = reciprocal_particle_weight[None, None, :]
    steps_all = companion_group_indices.shape[0] - 1
    swap_at = steps_all // 2
    push_vectors, energy, extended = force_from(
        starting_locations, interaction_strength, companion_group_indices, 0
    )
    saved_extended = [extended]
    saved_updated = []
    saved_factor = []
    saved_current = []
    stored_goal = []
    particle_location, particle_speed = (starting_locations, starting_speeds)
    desired_heat_level = heat_levels
    partner_temp = from_partner(heat_levels, "rep", 0)
    upcoming_heat_level = jnp.where(swap_indicator == 1, partner_temp, heat_levels)
    interaction_multiplier = jnp.sqrt(upcoming_heat_level / heat_levels)[:, None, None]
    for iteration_number in range(steps_all):
        if iteration_number == swap_at:
            particle_speed = particle_speed * interaction_multiplier
            desired_heat_level = upcoming_heat_level
        mid_velocity = particle_speed + half_step * mass_row * push_vectors
        particle_location = particle_location + TIME_STEP * mid_velocity
        push_vectors, energy, extended = force_from(
            particle_location, interaction_strength, companion_group_indices, iteration_number + 1
        )
        updated = mid_velocity + half_step * mass_row * push_vectors
        kinetic, energy = atom_total(
            (0.5 * jnp.sum(updated * updated / mass_row, axis=(1, 2)), energy)
        )
        present_state = 2.0 * kinetic / (3 * atoms_all) + KINETIC_EPSILON
        rescaling_multiplier = jnp.sqrt(
            1.0 + THERMO_RELAX * (desired_heat_level / present_state - 1.0)
        )
        particle_speed = rescaling_multiplier[:, None, None] * updated
        saved_extended.append(extended)
        saved_updated.append(updated)
        saved_factor.append(rescaling_multiplier)
        saved_current.append(present_state)
        stored_goal.append(desired_heat_level)
    energies = energy / atoms_all
    cot_x, cot_v = (terminal_location_adjoint, terminal_speed_adjoint)
    cot_f = jnp.zeros_like(cot_x)
    cot_coupling = jnp.zeros_like(interaction_strength)
    for iteration_number in reversed(range(steps_all)):
        updated = saved_updated[iteration_number]
        rescaling_multiplier = saved_factor[iteration_number]
        present_state = saved_current[iteration_number]
        desired_heat_level = stored_goal[iteration_number]
        inner_sum = atom_total(jnp.sum(cot_v * updated, axis=(1, 2)))
        slope_factor = (
            -THERMO_RELAX
            * desired_heat_level
            / (present_state * present_state)
            * (2.0 / (3 * atoms_all))
            / (2.0 * rescaling_multiplier)
        )
        cot_updated = (
            rescaling_multiplier[:, None, None] * cot_v
            + (inner_sum * slope_factor)[:, None, None] * updated / mass_row
        )
        cot_force_now = cot_f + half_step * mass_row * cot_updated
        returned_x, returned_c = force_back(
            cot_force_now,
            saved_extended[iteration_number + 1],
            companion_group_indices,
            iteration_number + 1,
        )
        cot_coupling = cot_coupling + returned_c
        cot_x = cot_x + returned_x
        cot_mid = cot_updated + TIME_STEP * cot_x
        cot_v = cot_mid
        cot_f = half_step * mass_row * cot_mid
        if iteration_number == swap_at:
            cot_v = cot_v * interaction_multiplier
    returned_x, returned_c = force_back(cot_f, saved_extended[0], companion_group_indices, 0)
    cot_x = cot_x + returned_x
    cot_coupling = cot_coupling + returned_c
    grad_coupling = lax.psum(cot_coupling, "rep")
    return (particle_location, particle_speed, energies, cot_x, cot_v, grad_coupling)


LOG2E = math.log2(math.e)
ROWS = 16
KDIST = 16
KCROSS = 32
KEPT = 8
UNROLL = 8


def split2(x):
    hi = x.astype(jnp.bfloat16).astype(jnp.float32)
    return hi, (x - hi).astype(jnp.bfloat16).astype(jnp.float32)


def row_sum(x):
    return jnp.sum(x, axis=1, keepdims=True)


def whole_sum(x):
    return jnp.full((1, x.shape[-1]), jnp.sum(x), jnp.float32)


def replica_kernel(
    far_ref,
    temp_ref,
    x0_ref,
    v0_ref,
    cx_ref,
    cv_ref,
    c_ref,
    m_ref,
    xf_ref,
    vf_ref,
    en_ref,
    gx_ref,
    gv_ref,
    gc_ref,
    left,
    right,
    left_w,
    right_w,
    rows_w,
    rows_x,
    rows_g,
    weights,
    acc_w,
    acc_v,
    out_w,
    out_v,
    saved_u,
    saved_x,
    f_ref,
    fac_ref,
    cur_ref,
):
    owners, _, atoms = x0_ref.shape
    nb, _, width = f_ref.shape
    blocks = nb // owners
    evals = rows_x.shape[0]
    steps = evals - 1
    partners = 2
    half = 0.5 * TIME_STEP
    block_count = blocks
    dof = float(3 * nb * width)
    f32, bf16 = jnp.float32, jnp.bfloat16
    real = slice(0, nb)
    t_first = temp_ref[0:1]
    t_last = temp_ref[1:2]
    swap_gain = jnp.sqrt(t_last / t_first)
    strength = 0.5 * block_count / (8.0 * partners)
    log_scale = math.log2(strength)

    def whole(ref):
        return jnp.stack(
            [
                ref[o, :, j * width : (j + 1) * width]
                for o in range(owners)
                for j in range(blocks)
            ]
        )

    def give(ref, value):
        for o in range(owners):
            for j in range(blocks):
                ref[o, :, j * width : (j + 1) * width] = value[o * blocks + j]

    def far(n, p, k):
        return far_ref[p // blocks, (n * partners + k) * blocks + p % blocks]

    mass = whole(m_ref)
    coupling = whole(c_ref)

    for ref in (left_w, right_w, rows_w):
        ref[...] = jnp.zeros_like(ref)
    rows_x[...] = jnp.zeros_like(rows_x)
    rows_g[...] = jnp.zeros_like(rows_g)

    def put(ref, at, value):
        ref[real, at : at + value.shape[1], :] = value

    one = jnp.ones((nb, 1, width), f32)
    zero_pad = (((0,), (0,)), ((), ()))

    def pair(ref, n, p):
        return jnp.concatenate([ref[far(n, p, k)] for k in range(partners)], axis=1)

    def scatter(out, acc, n):
        for p in range(nb):
            for k in range(partners):
                q = far(n, p, k)
                acc[q] = acc[q] + out[p, :, k * width : (k + 1) * width]

    def set_rows(dest, value):
        hi, low = split2(value)
        put(rows_w, 0, hi)
        put(rows_w, 3, low)
        put(rows_w, 6, one)
        dest[...] = rows_w[...].astype(bf16)

    def products(first, second, at):
        for i, j in ((0, 0), (0, 1), (1, 0)):
            put(left_w, at, first[i])
            put(right_w, at, second[j])
            at += first[0].shape[1]
        return at

    def singles(ref, other, value, at):
        for part in split2(value):
            put(ref, at, part)
            put(other, at, one)
            at += 1
        return at

    def force(x, n):
        set_rows(rows_x.at[n], x)
        saved_x[n] = x
        self_term = -0.5 * LOG2E * row_sum(x * x) + jnp.log(coupling) * LOG2E
        at = products(split2(x * LOG2E), split2(x), 0)
        at = singles(left_w, right_w, self_term + log_scale, at)
        at = singles(right_w, left_w, self_term, at)
        right_w[nb, at - 2 : at - 1, :] = jnp.full((1, width), -1e6, f32)
        left[:, 0:KDIST, :] = left_w[real, 0:KDIST, :].astype(bf16)
        right[:, 0:KDIST, :] = right_w[:, 0:KDIST, :].astype(bf16)

        @pl.loop(0, nb // UNROLL)
        def _(chunk):
            for i in range(UNROLL):
                p = chunk * UNROLL + i
                exponent = lax.dot_general(
                    left[p, 0:KDIST, :],
                    pair(right.at[:, 0:KDIST, :], n, p),
                    zero_pad,
                    preferred_element_type=f32,
                )
                w = jnp.exp2(exponent).astype(bf16)
                weights[n, p] = w
                out_w[p] = jnp.dot(rows_x[n, p], w, preferred_element_type=f32)[:KEPT]
                acc_w[p] = lax.dot_general(
                    pair(rows_x.at[n], n, p),
                    w,
                    (((1,), (1,)), ((), ())),
                    preferred_element_type=f32,
                )[:KEPT]

        scatter(out_w, acc_w, n)
        pulled = acc_w[real, 0:3, :] + acc_w[real, 3:6, :]
        f_ref[...] = x * acc_w[real, 6:7, :] - pulled

    def force_back(g, n):
        x = saved_x[n]
        set_rows(rows_g, g)
        sx, sg = split2(x), split2(g)
        neg_g = tuple(-part for part in sg)
        neg_x = tuple(-part for part in sx)
        at = products(sx, neg_g, 0)
        at = products(sg, neg_x, at)
        own = row_sum(x * g)
        at = singles(left_w, right_w, own, at)
        singles(right_w, left_w, own, at)
        left[...] = left_w[real].astype(bf16)
        right[...] = right_w[...].astype(bf16)

        @pl.loop(0, nb // UNROLL)
        def _(chunk):
            for i in range(UNROLL):
                p = chunk * UNROLL + i
                phi = lax.dot_general(
                    left[p], pair(right, n, p), zero_pad, preferred_element_type=f32
                )
                w = weights[n, p]
                v = (w.astype(f32) * phi).astype(bf16)
                out_w[p] = jnp.dot(rows_g[p], w, preferred_element_type=f32)[:KEPT]
                out_v[p] = jnp.dot(rows_x[n, p], v, preferred_element_type=f32)[:KEPT]
                acc_w[p] = lax.dot_general(
                    pair(rows_g, n, p),
                    w,
                    (((1,), (1,)), ((), ())),
                    preferred_element_type=f32,
                )[:KEPT]
                acc_v[p] = lax.dot_general(
                    pair(rows_x.at[n], n, p),
                    v,
                    (((1,), (1,)), ((), ())),
                    preferred_element_type=f32,
                )[:KEPT]

        scatter(out_w, acc_w, n)
        scatter(out_v, acc_v, n)
        pulled_w = acc_w[real, 0:3, :] + acc_w[real, 3:6, :]
        pulled_v = acc_v[real, 0:3, :] + acc_v[real, 3:6, :]
        total_v = acc_v[real, 6:7, :]
        back_x = g * acc_w[real, 6:7, :] - pulled_w - x * total_v + pulled_v
        return back_x, total_v

    x, v, goal = whole(x0_ref), whole(v0_ref), t_first
    force(x, 0)
    for n in range(steps):
        if n == steps // 2:
            v = v * swap_gain
            goal = t_last
        mid = v + half * mass * f_ref[...]
        x = x + TIME_STEP * mid
        force(x, n + 1)
        u = mid + half * mass * f_ref[...]
        kinetic = 0.5 * whole_sum(u * u / mass)
        current = 2.0 * kinetic / dof + KINETIC_EPSILON
        factor = jnp.sqrt(1.0 + THERMO_RELAX * (goal / current - 1.0))
        v = factor * u
        saved_u[n] = u
        fac_ref[n] = factor
        cur_ref[n] = current
    give(xf_ref, x)
    give(vf_ref, v)
    selfs = jnp.zeros((1, width), f32)
    square = strength * jnp.sum(coupling * coupling, axis=1)
    for p in range(nb):
        for k in range(partners):
            hit = (far(steps, p, k) == p).astype(f32)
            selfs = selfs + hit * square[p : p + 1]
    total = whole_sum(acc_w[real, 6:7, :]) * 0.5 - whole_sum(selfs)
    en_ref[...] = total / float(nb * width)

    cot_x, cot_v = whole(cx_ref), whole(cv_ref)
    cot_f = jnp.zeros_like(cot_x)
    cot_c = jnp.zeros((nb, 1, width), f32)
    for n in reversed(range(steps)):
        goal = t_last if n >= steps // 2 else t_first
        u, factor, current = saved_u[n], fac_ref[n], cur_ref[n]
        inner = whole_sum(cot_v * u)
        slope = -THERMO_RELAX * goal / (current * current) * (2.0 / dof) / (2.0 * factor)
        cot_u = factor * cot_v + (inner * slope) * u / mass
        back_x, back_c = force_back(cot_f + half * mass * cot_u, n + 1)
        cot_c = cot_c + back_c
        cot_x = cot_x + back_x
        cot_mid = cot_u + TIME_STEP * cot_x
        cot_v = cot_mid
        cot_f = half * mass * cot_mid
        if n == steps // 2:
            cot_v = cot_v * swap_gain
    back_x, back_c = force_back(cot_f, 0)
    give(gx_ref, cot_x + back_x)
    give(gv_ref, cot_v)
    give(gc_ref, (cot_c + back_c) / coupling)


def run_replica(far, temps, x0, v0, cx, cv, coupling, mass, evals, blocks):
    owners, _, atoms = x0.shape
    nb, width = owners * blocks, atoms // blocks
    f32, bf16 = jnp.float32, jnp.bfloat16
    vec = jax.ShapeDtypeStruct((owners, 3, atoms), f32)
    vmem = pl.BlockSpec(memory_space=pltpu.VMEM)
    smem = pl.BlockSpec(memory_space=pltpu.SMEM)
    return pl.pallas_call(
        replica_kernel,
        out_shape=(
            vec,
            vec,
            jax.ShapeDtypeStruct((1, width), f32),
            vec,
            vec,
            jax.ShapeDtypeStruct((owners, 1, atoms), f32),
        ),
        in_specs=[smem] + [vmem] * 7,
        out_specs=[vmem] * 6,
        scratch_shapes=[
            pltpu.VMEM((nb, KCROSS, width), bf16),
            pltpu.VMEM((nb + 1, KCROSS, width), bf16),
            pltpu.VMEM((nb + 1, KCROSS, width), f32),
            pltpu.VMEM((nb + 1, KCROSS, width), f32),
            pltpu.VMEM((nb + 1, ROWS, width), f32),
            pltpu.VMEM((evals, nb + 1, ROWS, width), bf16),
            pltpu.VMEM((nb + 1, ROWS, width), bf16),
            pltpu.VMEM((evals, nb, width, 2 * width), bf16),
            pltpu.VMEM((nb + 1, KEPT, width), f32),
            pltpu.VMEM((nb + 1, KEPT, width), f32),
            pltpu.VMEM((nb, KEPT, 2 * width), f32),
            pltpu.VMEM((nb, KEPT, 2 * width), f32),
            pltpu.VMEM((evals - 1, nb, 3, width), f32),
            pltpu.VMEM((evals, nb, 3, width), f32),
            pltpu.VMEM((nb, 3, width), f32),
            pltpu.VMEM((evals - 1, 1, width), f32),
            pltpu.VMEM((evals - 1, 1, width), f32),
        ],
        compiler_params=pltpu.CompilerParams(vmem_limit_bytes=60 * 1024 * 1024),
    )(far, temps, x0, v0, cx, cv, coupling, mass)


MESH = pl.DeviceIdType.MESH


def greet(peers):
    barrier = pltpu.get_barrier_semaphore()
    for peer in peers:
        pl.semaphore_signal(barrier, inc=1, device_id=peer, device_id_type=MESH)
    pl.semaphore_wait(barrier, len(peers))


def others(axis):
    me, count = lax.axis_index(axis), lax.axis_size(axis)
    return [lax.rem(me + d, count) for d in range(1, count)]


def entry_kernel(blocks, partners, *refs):
    ins, outs = refs[:9], refs[9:17]
    stage = refs[17:21]
    heat_in, send_sem, recv_sem, heat_send, heat_recv = refs[21:]
    heat_ref, flag_ref = ins[7:]
    temp_ref = outs[7]
    me, owners = lax.axis_index("atom"), lax.axis_size("atom")
    rep = lax.axis_index("rep")
    partner = rep + 1 - 2 * lax.rem(rep, 2)
    peers = others("atom")
    for i in range(4):
        for r in range(owners):
            stage[i][r] = ins[i][:, r, :]
    twin = {"rep": partner, "atom": me}
    greet([{"rep": rep, "atom": peer} for peer in peers] + [twin])
    heat_copy = pltpu.make_async_remote_copy(
        src_ref=heat_ref,
        dst_ref=heat_in,
        send_sem=heat_send,
        recv_sem=heat_recv,
        device_id=twin,
        device_id_type=MESH,
    )
    heat_copy.start()
    copies = []
    for d, peer in enumerate(peers):
        for i in range(7):
            copies.append(
                pltpu.make_async_remote_copy(
                    src_ref=stage[i].at[peer] if i < 4 else ins[i],
                    dst_ref=outs[i].at[me],
                    send_sem=send_sem.at[d, i],
                    recv_sem=recv_sem.at[d, i],
                    device_id={"rep": rep, "atom": peer},
                    device_id_type=MESH,
                )
            )
            copies[-1].start()
    for i in range(7):
        outs[i][me] = stage[i][me] if i < 4 else ins[i][...]
    heat_copy.wait()
    own = heat_ref[...]
    upcoming = jnp.where(flag_ref[...] == 1, heat_in[...], own)
    lane = lax.broadcasted_iota(jnp.int32, own.shape, 1)
    for row, value in enumerate((own, upcoming)):
        chosen = jnp.sum(jnp.where(lane == me, value, 0.0), axis=1, keepdims=True)
        temp_ref[row : row + 1, :] = jnp.broadcast_to(chosen, (1, temp_ref.shape[1]))
    for copy in copies:
        copy.wait()
    slots = outs[6][...]
    owner = lax.broadcasted_iota(jnp.int32, slots.shape, 0)
    block = slots + (owner - 1) * blocks
    inside = (block >= 0) & (block < owners * blocks)
    outs[6][...] = jnp.where(inside, block, owners * blocks)


def exit_kernel(*refs):
    ins, outs = refs[:6], refs[6:12]
    land = refs[12:16]
    en_in, gc_in, rep_in, total, send_sem, recv_sem, rep_send, rep_recv = refs[16:]
    en_ref, gc_ref = ins[4], ins[5]
    me, rep = lax.axis_index("atom"), lax.axis_index("rep")
    peers, rep_peers = others("atom"), others("rep")
    greet(
        [{"rep": rep, "atom": peer} for peer in peers]
        + [{"rep": peer, "atom": me} for peer in rep_peers]
    )
    dests = (gc_in,) + tuple(land) + (en_in,)
    sources = (gc_ref,) + tuple(ins[:4]) + (en_ref,)
    copies = {}
    for i in range(6):
        for d, peer in enumerate(peers):
            copies[d, i] = pltpu.make_async_remote_copy(
                src_ref=sources[i].at[peer] if i < 5 else sources[i],
                dst_ref=dests[i].at[me] if i else gc_in.at[d],
                send_sem=send_sem.at[d, i],
                recv_sem=recv_sem.at[d, i],
                device_id={"rep": rep, "atom": peer},
                device_id_type=MESH,
            )
            copies[d, i].start()
    part = gc_ref[me]
    for d in range(len(peers)):
        copies[d, 0].wait()
        part = part + gc_in[d]
    total[...] = part
    rep_copies = []
    for d, peer in enumerate(rep_peers):
        rep_copies.append(
            pltpu.make_async_remote_copy(
                src_ref=total,
                dst_ref=rep_in.at[d],
                send_sem=rep_send.at[d],
                recv_sem=rep_recv.at[d],
                device_id={"rep": peer, "atom": me},
                device_id_type=MESH,
            )
        )
        rep_copies[-1].start()
    for i in range(4):
        land[i][me] = ins[i][me]
    en_in[me] = en_ref[...]
    for d in range(len(peers)):
        for i in range(1, 6):
            copies[d, i].wait()
    for i in range(4):
        for r in range(lax.axis_size("atom")):
            outs[i][:, r, :] = land[i][r]
    lane = lax.broadcasted_iota(jnp.int32, en_ref.shape, 1)
    energies = jnp.zeros(en_ref.shape, jnp.float32)
    for r in range(lax.axis_size("atom")):
        energies = jnp.where(lane == r, en_in[r], energies)
    outs[4][...] = energies[:, : outs[4].shape[1]]
    for d, copy in enumerate(rep_copies):
        copy.wait()
        part = part + rep_in[d]
    outs[5][...] = part


def enter(split, shared, heat, flags, blocks, partners, lanes):
    f32 = jnp.float32
    moved = [(a.shape[1], a.shape[0], a.shape[2]) for a in split]
    owners = lax.axis_size("atom")
    vmem = pl.BlockSpec(memory_space=pltpu.VMEM)
    dma = pltpu.SemaphoreType.DMA
    return pl.pallas_call(
        functools.partial(entry_kernel, blocks, partners),
        out_shape=tuple(jax.ShapeDtypeStruct(s, f32) for s in moved)
        + tuple(jax.ShapeDtypeStruct((owners,) + a.shape, a.dtype) for a in shared)
        + (jax.ShapeDtypeStruct((2, lanes), f32),),
        in_specs=[vmem] * 9,
        out_specs=[vmem] * 8,
        scratch_shapes=[pltpu.VMEM(s, f32) for s in moved]
        + [
            pltpu.VMEM(heat.shape, f32),
            dma((owners - 1, 7)),
            dma((owners - 1, 7)),
            dma,
            dma,
        ],
        compiler_params=pltpu.CompilerParams(collective_id=0, has_side_effects=True),
    )(*split, *shared, heat, flags)


def leave(xf, vf, gx, gv, en, gc):
    f32 = jnp.float32
    owners, reps = lax.axis_size("atom"), lax.axis_size("rep")
    vmem = pl.BlockSpec(memory_space=pltpu.VMEM)
    dma = pltpu.SemaphoreType.DMA
    vec = jax.ShapeDtypeStruct((xf.shape[1], owners, xf.shape[2]), f32)
    return pl.pallas_call(
        exit_kernel,
        out_shape=(vec, vec, vec, vec)
        + (
            jax.ShapeDtypeStruct((1, owners), f32),
            jax.ShapeDtypeStruct(gc.shape[1:], f32),
        ),
        in_specs=[vmem] * 6,
        out_specs=[vmem] * 6,
        scratch_shapes=[pltpu.VMEM(xf.shape, f32)] * 4
        + [
            pltpu.VMEM((owners,) + en.shape, f32),
            pltpu.VMEM((owners - 1,) + gc.shape[1:], f32),
            pltpu.VMEM((reps - 1,) + gc.shape[1:], f32),
            pltpu.VMEM(gc.shape[1:], f32),
            dma((owners - 1, 6)),
            dma((owners - 1, 6)),
            dma((reps - 1,)),
            dma((reps - 1,)),
        ],
        compiler_params=pltpu.CompilerParams(collective_id=1, has_side_effects=True),
    )(xf, vf, gx, gv, en, gc)


def local_whole(
    starting_locations,
    starting_speeds,
    terminal_location_adjoint,
    terminal_speed_adjoint,
    interaction_strength,
    reciprocal_particle_weight,
    heat_levels,
    swap_indicator,
    companion_group_indices,
):
    evals, blocks, partners = companion_group_indices.shape
    lanes = starting_locations.shape[2] // blocks

    def turned(x):
        return x.transpose(1, 0, 2)

    *mine, coupling, mass, far, temps = enter(
        tuple(
            turned(x)
            for x in (
                starting_locations,
                starting_speeds,
                terminal_location_adjoint,
                terminal_speed_adjoint,
            )
        ),
        (
            interaction_strength.reshape(1, -1),
            reciprocal_particle_weight.reshape(1, -1),
            companion_group_indices.transpose(0, 2, 1),
        ),
        heat_levels.reshape(1, -1),
        swap_indicator.reshape(1, -1),
        blocks,
        partners,
        lanes,
    )
    xf, vf, en, gx, gv, gc = run_replica(
        far.reshape(far.shape[0], -1), temps, *mine, coupling, mass, evals, blocks
    )
    xf, vf, gx, gv, energies, grad_coupling = leave(xf, vf, gx, gv, en, gc)
    return (
        turned(xf),
        turned(vf),
        energies[0],
        turned(gx),
        turned(gv),
        grad_coupling.reshape(-1),
    )


def local(*args):
    partners = args[8].shape[2]
    fits = args[0].shape[0] == lax.axis_size("atom") and partners == 2
    if fits and lax.axis_size("rep") % 2 == 0:
        return local_whole(*args)
    return local_general(*args)


def solution(mesh):
    in_specs = (
        P("rep", None, "atom"),
        P("rep", None, "atom"),
        P("rep", None, "atom"),
        P("rep", None, "atom"),
        P("atom"),
        P("atom"),
        P("rep"),
        P("rep"),
        P(None, "atom", None),
    )
    out_specs = (
        P("rep", None, "atom"),
        P("rep", None, "atom"),
        P("rep"),
        P("rep", None, "atom"),
        P("rep", None, "atom"),
        P("atom"),
    )
    return jax.shard_map(local, mesh=mesh, in_specs=in_specs, out_specs=out_specs, check_vma=False)
```
